256 devices in a mesh: tile: 32 (over x, z), lev: 8 (over y, core).
Axes of the slice: x: 4, y: 4, z: 8, core: 2. Of those that a mesh axis runs over, the one named last changes fastest.
Arguments:
- krylov: bfloat16 [4, 16, 5, 8192, 128], P(None, 'lev', None, 'tile'), may hold values from -7 to 7, as said below
- adjoint: float32 [16, 5, 8192, 128], P('lev', None, 'tile'), may hold values from -200 to 200
- projected: float32 [4, 4], replicated, may hold values from -3 to 3
- stencil: bfloat16 [5, 16, 8192, 128], P(None, 'lev', 'tile'), may hold values from 0.19921875 to 1
- column_weight: float32 [2, 16, 8192, 128], P(None, 'lev', 'tile'), may hold values from 0.05 to 0.3
- seam_turns: int32 [32, 4], P('tile'), may hold values from 0 to 3
Outputs:
- updated: float32 [16, 5, 8192, 128], P('lev', None, 'tile')
The draws below stay inside these ranges and needn't reach their ends.
Inputs may be any that keep to these rules, and one draw needn't show every extreme that they name: `krylov`: krylov vectors of order one.
All inputs are finite; a program needn't handle non-finite values.
Results may differ from the reference program's by a relative error of at most 0.0003.
Values sent between devices are 32-bit elements; how exact they have to be, the bound alone decides.
A program may use at most 128 MiB of HBM per device.

```python
import math
import jax
import jax.numpy as jnp

FIELDS = 5
KRYLOV = 4
STRIDE = 4
HX = 256
HY = 128
TILES = 32
LEVELS = 16
ROWS = 8192


def shared_basis(key):
    return jax.random.normal(jax.random.fold_in(key, 11), (KRYLOV, LEVELS, FIELDS, ROWS, HY), jnp.float32)


def draw_krylov(key, part):
    return shared_basis(key).astype(jnp.bfloat16)


def draw_adjoint(key, part):
    basis_all = shared_basis(key)
    factors = jax.random.uniform(jax.random.fold_in(key, 12), (KRYLOV,), jnp.float32, -1.0, 1.0)
    blended = jnp.zeros((LEVELS, FIELDS, ROWS, HY), jnp.float32)
    for k in range(KRYLOV):
        blended = blended + 0.5 * factors[k] * basis_all[k]
    log_amp = jax.random.uniform(jax.random.fold_in(key, 14), (LEVELS, TILES), jnp.float32, -2.0794415, 2.0794415)
    amplitude = jnp.repeat(jnp.exp(log_amp), HX, axis=1)
    tile_rise = 1.0 + 2.0 * (jnp.arange(ROWS) // HX).astype(jnp.float32) / (TILES - 1)
    noise = jax.random.normal(jax.random.fold_in(key, 13), (LEVELS, FIELDS, ROWS, HY), jnp.float32)
    level_rise = 1.0 + 0.5 * jnp.arange(LEVELS).astype(jnp.float32) / (LEVELS - 1)
    rough = noise * tile_rise[None, None, :, None] * level_rise[:, None, None, None]
    return blended * amplitude[:, None, :, None] + rough


def with_ends(entries, stream_key, smallest, top_value):
    place = [jax.random.randint(jax.random.fold_in(stream_key, axis), (), 0, length) for axis, length in enumerate(entries.shape)]
    main_axis = entries.shape.index(max(entries.shape))
    neighbour = place[:main_axis] + [(place[main_axis] + 1) % entries.shape[main_axis]] + place[main_axis + 1:]
    return entries.at[tuple(place)].set(smallest).at[tuple(neighbour)].set(top_value)


def block_scale(rng, dims, shards, least, high):
    loudness = 1.0
    for position, blocks in shards:
        steps = jax.random.uniform(jax.random.fold_in(jax.random.fold_in(rng, 6), position), (blocks,), jnp.float32, least / len(shards), high / len(shards))
        loudness = loudness * jnp.repeat(jnp.exp(steps), dims[position] // blocks).reshape((-1,) + (1,) * (len(dims) - 1 - position))
    return loudness


def normal_values(stream_key, dims, deviation, limit, held_as=jnp.bfloat16):
    return jnp.clip(deviation * jax.random.normal(stream_key, dims, jnp.float32), -limit, limit).astype(held_as)


def setup_inputs(seed: int = 0) -> dict:
    arg_keys = jax.random.split(jax.random.key(seed), 7)
    krylov = draw_krylov(jax.random.fold_in(arg_keys[6], 71), 0)
    adjoint = draw_adjoint(jax.random.fold_in(arg_keys[6], 71), 0)
    projected = normal_values(arg_keys[2], (KRYLOV, KRYLOV), 1.0, 3.0, jnp.float32)
    stencil = jnp.clip(jnp.exp(math.log(1.0) - 1.6133518 * jax.random.uniform(arg_keys[3], (5, LEVELS, ROWS, HY), jnp.float32) ** block_scale(arg_keys[3], (5, LEVELS, ROWS, HY), ((1, 8), (2, 32)), -0.2, 0.2)), 0.19921875, 1.0).astype(jnp.bfloat16)
    column_weight = jnp.clip(jnp.exp(math.log(0.3) - 1.7917595 * jax.random.uniform(arg_keys[4], (2, LEVELS, ROWS, HY), jnp.float32) ** block_scale(arg_keys[4], (2, LEVELS, ROWS, HY), ((1, 8), (2, 32)), -0.2, 0.2)), 0.05, 0.3)
    seam_turns = with_ends(jax.random.randint(arg_keys[5], (TILES, 4), 0, 4), jax.random.fold_in(arg_keys[5], 1), 0, 3).astype(jnp.int32)
    return {"krylov": krylov, "adjoint": adjoint, "projected": projected, "stencil": stencil, "column_weight": column_weight, "seam_turns": seam_turns}


def rotate(edge_strip, turning):
    flipped = jnp.where(turning % 2 == 1, edge_strip[..., ::-1], edge_strip)
    cosine = jnp.where(turning == 0, 1.0, jnp.where(turning == 2, -1.0, 0.0)).astype(edge_strip.dtype)
    sine_part = jnp.where(turning == 1, 1.0, jnp.where(turning == 3, -1.0, 0.0)).astype(edge_strip.dtype)
    wind_east = flipped[..., 2:3, :]
    wind_north = flipped[..., 3:4, :]
    turned_u = cosine * wind_east - sine_part * wind_north
    turned_v = sine_part * wind_east + cosine * wind_north
    return jnp.concatenate([flipped[..., :2, :], turned_u, turned_v, flipped[..., 4:, :]], axis=-2)


def reference(krylov, adjoint, projected, stencil, column_weight, seam_turns):
    count = LEVELS * FIELDS * ROWS * HY
    coupling = jnp.stack([jnp.sum(krylov[k].astype(jnp.float32) * adjoint) for k in range(KRYLOV)]) / count
    mixing = jnp.sum(projected * coupling[:, None], axis=0)
    combined = jnp.zeros(adjoint.shape, jnp.float32)
    for k in range(KRYLOV):
        combined = combined + mixing[k] * krylov[k].astype(jnp.float32)
    field = jnp.transpose(combined.reshape(LEVELS, FIELDS, TILES, HX, HY), (2, 0, 1, 3, 4))
    coeffs = jnp.transpose(stencil.astype(jnp.float32).reshape(5, LEVELS, TILES, HX, HY), (0, 2, 1, 3, 4))[:, :, :, None]
    turning = [seam_turns[:, s][:, None, None, None] for s in range(4)]
    image = coeffs[0] * field
    plus_rows = coeffs[1] * field
    rim_strip = rotate(jnp.roll(plus_rows[..., -1, :], 1, axis=0), turning[0])
    image = image + jnp.concatenate([rim_strip[..., None, :], plus_rows[..., :-1, :]], axis=-2)
    minus_rows = coeffs[2] * field
    rim_strip = rotate(jnp.roll(minus_rows[..., 0, :], -1, axis=0), turning[1])
    image = image + jnp.concatenate([minus_rows[..., 1:, :], rim_strip[..., None, :]], axis=-2)
    plus_cols = coeffs[3] * field
    rim_strip = rotate(jnp.roll(plus_cols[..., -1], STRIDE, axis=0), turning[2])
    image = image + jnp.concatenate([rim_strip[..., None], plus_cols[..., :-1]], axis=-1)
    minus_cols = coeffs[4] * field
    rim_strip = rotate(jnp.roll(minus_cols[..., 0], -STRIDE, axis=0), turning[3])
    image = image + jnp.concatenate([minus_cols[..., 1:], rim_strip[..., None]], axis=-1)
    weights = jnp.transpose(column_weight.reshape(2, LEVELS, TILES, HX, HY), (0, 2, 1, 3, 4))
    pressure_sum = jnp.cumsum(field[:, ::-1, 0], axis=1)[:, ::-1]
    height_sum = jnp.cumsum(field[:, ::-1, 3], axis=1)[:, ::-1]
    zeros_part = jnp.zeros_like(pressure_sum)
    column_part = jnp.stack([zeros_part, weights[0] * pressure_sum, zeros_part, zeros_part, weights[1] * height_sum], axis=2)
    image = image + column_part
    image = jnp.transpose(image, (1, 2, 0, 3, 4)).reshape(LEVELS, FIELDS, ROWS, HY)
    return adjoint + 0.5 * image
```

```python
import functools

import jax
import jax.numpy as jnp
from jax import lax
from jax.experimental import pallas as pl
from jax.experimental.pallas import tpu as pltpu
from jax.sharding import PartitionSpec as P

MESH = pl.DeviceIdType.MESH
STRIDE = 4
KRYLOV = 4
FIELDS = 5
LEVELS = 2
ROWS = 256
COLS = 128
HALF = ROWS // 2
CHUNKS = 4
PART = 2 * HALF // CHUNKS
NX, NZ, NY, NC = 4, 8, 4, 2
PAIRS = LEVELS * FIELDS
COUNT = 16 * FIELDS * 8192 * COLS


def ring(d, n):
    return min(d % n, (-d) % n)


GROUP_XY = sorted(
    [(dx, dy) for dx in range(NX) for dy in range(NY) if (dx, dy) != (0, 0)],
    key=lambda o: -(ring(o[0], NX) + ring(o[1], NY)),
)
GROUP_ZC = sorted(
    [(dz, dc) for dz in range(NZ) for dc in range(NC) if (dz, dc) != (0, 0)],
    key=lambda o: -(ring(o[0], NZ) + 0.5 * o[1]),
)


def splat_sum(x):
    return jnp.sum(jnp.sum(x, axis=0, keepdims=True), axis=1, keepdims=True)


def turned(strip, turn, lane_flip):
    odd = lax.rem(turn, 2) == 1
    cosine = jnp.where(turn == 0, 1.0, jnp.where(turn == 2, -1.0, 0.0)).astype(jnp.float32)
    sine = jnp.where(turn == 1, 1.0, jnp.where(turn == 3, -1.0, 0.0)).astype(jnp.float32)
    halves = [strip[:, i : i + COLS] for i in range(0, strip.shape[1], COLS)]
    back = [jnp.take_along_axis(h, lane_flip, axis=1) for h in halves[::-1]]
    pair = lax.broadcasted_iota(jnp.int32, halves[0].shape, 0)
    field = lax.rem(pair, FIELDS)
    out = []
    for h, b in zip(halves, back):
        x = jnp.where(odd, b, h)
        after = pltpu.roll(x, x.shape[0] - 1, 0)
        before = pltpu.roll(x, 1, 0)
        out.append(
            jnp.where(
                field == 2,
                cosine * x - sine * after,
                jnp.where(field == 3, sine * before + cosine * x, x),
            )
        )
    return out


def kernel(
    k_hbm, a_hbm, s_hbm, w_hbm, proj, seam,
    out,
    kv, av, sv, wv, comb,
    ls_own, ls_send, ls_recv,
    total, mine, other, relay, buf_a, buf_b, below_send, below,
    row1, row2, got1, got2,
    row_send, row_got, col_mix, col_t, col_send, col_got, col_back, col_add,
    load_sem, red_send, red_recv, ls_sem, y_send, a_sem, b_sem, below_sem, edge_sem,
):
    t, l = lax.axis_index("tile"), lax.axis_index("lev")
    x, z, y, c = t // NZ, lax.rem(t, NZ), l // NC, lax.rem(l, NC)
    f32 = jnp.float32

    loads = []
    for f in range(FIELDS):
        loads.append(pltpu.make_async_copy(k_hbm.at[:, :, f], kv.at[:, :, f], load_sem.at[f]))
        loads.append(pltpu.make_async_copy(a_hbm.at[:, f], av.at[:, f], load_sem.at[FIELDS + f]))
    load_s = pltpu.make_async_copy(s_hbm, sv, load_sem.at[2 * FIELDS])
    load_w = pltpu.make_async_copy(w_hbm, wv, load_sem.at[2 * FIELDS + 1])
    order = [0, 3, 1, 2, 4]
    for f in order:
        loads[2 * f].start()
        loads[2 * f + 1].start()

    def at_xy(dx, dy):
        return (lax.rem(x + dx, NX) * NZ + z, lax.rem(y + dy, NY) * NC + c)

    def at_zc(dz, dc):
        return (x * NZ + lax.rem(z + dz, NZ), y * NC + lax.rem(c + dc, NC))

    def at_tile(d):
        return (lax.rem(t + d + NX * NZ, NX * NZ), l)

    peers = [at_xy(*o) for o in GROUP_XY] + [at_zc(*o) for o in GROUP_ZC]
    peers += [at_tile(d) for d in (STRIDE, -STRIDE, 1, -1)]
    barrier = pltpu.get_barrier_semaphore()
    for peer in peers:
        pl.semaphore_signal(barrier, inc=1, device_id=peer, device_id_type=MESH)
    load_s.start()
    load_w.start()

    zero8 = jnp.zeros((8, COLS), f32)
    sums = (zero8,) * KRYLOV
    keep, give = c * HALF, (1 - c) * HALF
    for f in order:
        loads[2 * f].wait()
        loads[2 * f + 1].wait()

        def dots(i, sums, f=f):
            lev, blk = i // 16, lax.rem(i, 16)
            at = pl.ds(pl.multiple_of(blk * 16, 16), 16)
            a = av[lev, f, at, :]
            out_sums = []
            for k in range(KRYLOV):
                prod = kv[k, lev, f, at, :].astype(f32) * a
                out_sums.append(sums[k] + prod[0:8] + prod[8:16])
            return tuple(out_sums)

        sums = lax.fori_loop(0, LEVELS * 16, dots, sums, unroll=4)
        if f in (0, 3):
            g = f // 3

            def level_sums(k, _, f=f, g=g):
                for dst, start in ((ls_send, give), (ls_own, keep)):
                    at = pl.ds(pl.multiple_of(start, HALF), HALF)
                    dst[k, g] = kv[k, 0, f, at, :].astype(f32) + kv[k, 1, f, at, :].astype(f32)
                return 0

            lax.fori_loop(0, KRYLOV, level_sums, 0)

    lane1 = lax.broadcasted_iota(jnp.int32, (1, COLS), 1)
    mine_row = jnp.zeros((1, COLS), f32)
    for k in range(KRYLOV):
        mine_row = jnp.where(lane1 == k, splat_sum(sums[k]), mine_row)
    row1[...] = mine_row

    pl.semaphore_wait(barrier, len(peers))

    for j, o in enumerate(GROUP_XY):
        pltpu.make_async_remote_copy(
            src_ref=row1, dst_ref=got1.at[j], send_sem=red_send.at[0], recv_sem=red_recv.at[0],
            device_id=at_xy(*o), device_id_type=MESH,
        ).start()
    swap = pltpu.make_async_remote_copy(
        src_ref=ls_send, dst_ref=ls_recv, send_sem=ls_sem.at[0], recv_sem=ls_sem.at[1],
        device_id=at_zc(0, 1), device_id_type=MESH,
    )
    swap.start()
    pltpu.make_async_copy(got1, got1, red_recv.at[0]).wait()
    stage = row1[...]
    for j in range(len(GROUP_XY)):
        stage = stage + got1[j]
    row2[...] = stage
    for j, o in enumerate(GROUP_ZC):
        pltpu.make_async_remote_copy(
            src_ref=row2, dst_ref=got2.at[j], send_sem=red_send.at[1], recv_sem=red_recv.at[1],
            device_id=at_zc(*o), device_id_type=MESH,
        ).start()
    load_s.wait()
    load_w.wait()
    swap.wait()
    pltpu.make_async_copy(got1, got1, red_send.at[0]).wait()
    pltpu.make_async_copy(got2, got2, red_recv.at[1]).wait()
    stage = row2[...]
    for j in range(len(GROUP_ZC)):
        stage = stage + got2[j]
    coupling = [
        jnp.sum(jnp.where(lane1 == k, stage, 0.0), axis=1, keepdims=True) * (0.5 / COUNT)
        for k in range(KRYLOV)
    ]
    mix = []
    for j in range(KRYLOV):
        m = proj[0, j] * coupling[0]
        for k in range(1, KRYLOV):
            m = m + proj[k, j] * coupling[k]
        mix.append(jnp.broadcast_to(m, (8, COLS)))

    def mixed(parts):
        acc = None
        for m, p in zip(mix, parts):
            rows = p.shape[0]
            term = jnp.concatenate([m] * (rows // 8), axis=0) * p
            acc = term if acc is None else acc + term
        return acc

    for j in range(CHUNKS):
        g, at = (j * PART) // HALF, pl.ds((j * PART) % HALF, PART)
        m = mixed([ls_own[k, g, at, :] for k in range(KRYLOV)])
        o = mixed([ls_recv[k, g, at, :] for k in range(KRYLOV)])
        mine[j] = m
        other[j] = o
        total[j] = m + o

        def down(src, dst, slot, sem):
            return pltpu.make_async_remote_copy(
                src_ref=src, dst_ref=dst, send_sem=y_send.at[slot], recv_sem=sem,
                device_id=at_xy(0, NY - 1), device_id_type=MESH,
            )

        def up(src, dst, slot, sem):
            return pltpu.make_async_remote_copy(
                src_ref=src, dst_ref=dst, send_sem=y_send.at[slot], recv_sem=sem,
                device_id=at_xy(0, 1), device_id_type=MESH,
            )

        @pl.when(y >= 2)
        def _(j=j):
            down(total.at[j], buf_a.at[j], j, a_sem.at[j]).start()

        @pl.when(y == NY - 1)
        def _(j=j):
            up(total.at[j], buf_b.at[j], CHUNKS + j, b_sem.at[j]).start()

    def combine(i, _):
        for f in range(FIELDS):
            lev, blk = i // 8, lax.rem(i, 8)
            at = pl.ds(pl.multiple_of(blk * 32, 32), 32)
            comb[lev * FIELDS + f, at, :] = mixed(
                [kv[k, lev, f, at, :].astype(f32) for k in range(KRYLOV)]
            )
        return 0

    lax.fori_loop(0, LEVELS * 8, combine, 0)

    lane = lax.broadcasted_iota(jnp.int32, (ROWS, COLS), 1)
    for p in range(PAIRS):
        lev = p // FIELDS
        row_send[0, p : p + 1, :] = (
            sv[1, lev, ROWS - 16 : ROWS, :].astype(f32)[15:16] * comb[p, ROWS - 1 : ROWS, :]
        )
        row_send[1, p : p + 1, :] = sv[2, lev, 0:16, :].astype(f32)[0:1] * comb[p, 0:1, :]

    def strips(p, _):
        lev = p // FIELDS
        field = comb[p]
        both = jnp.where(
            lane == 0, sv[4, lev].astype(f32) * field, sv[3, lev].astype(f32) * field
        )
        moved = pltpu.roll(both, 2 * p + 1, 1)
        col_mix[...] = jnp.where(lane // 2 == p, moved, col_mix[...])
        return 0

    col_mix[...] = jnp.zeros((ROWS, COLS), f32)
    row_send[:, PAIRS:, :] = jnp.zeros((2, 16 - PAIRS, COLS), f32)
    lax.fori_loop(0, PAIRS, strips, 0)
    for i in range(2):
        col_t[...] = jnp.transpose(col_mix[i * COLS : (i + 1) * COLS, :])
        for s in range(2):
            col_send[s, :, i * COLS : (i + 1) * COLS] = col_t[pl.ds(s, 16, stride=2), :]

    edges = []
    for s, (src, dst, d) in enumerate(
        (
            (row_send.at[0], row_got.at[0], 1),
            (row_send.at[1], row_got.at[1], -1),
            (col_send.at[0], col_got.at[0], STRIDE),
            (col_send.at[1], col_got.at[1], -STRIDE),
        )
    ):
        edges.append(
            pltpu.make_async_remote_copy(
                src_ref=src, dst_ref=dst, send_sem=edge_sem.at[s], recv_sem=edge_sem.at[4 + s],
                device_id=at_tile(d), device_id_type=MESH,
            )
        )
    for s in (2, 3, 0, 1):
        edges[s].start()

    for j in range(CHUNKS):

        @pl.when(y == 1)
        def _(j=j):
            down(total.at[j], buf_a.at[j], j, a_sem.at[j]).wait_recv()
            relay[j] = total[j] + buf_a[j]
            down(relay.at[j], buf_a.at[j], j, a_sem.at[j]).start()

        @pl.when(y == 0)
        def _(j=j):
            up(total.at[j], buf_b.at[j], CHUNKS + j, b_sem.at[j]).wait_recv()
            up(buf_b.at[j], buf_b.at[j], CHUNKS + j, b_sem.at[j]).start()

    row = lax.broadcasted_iota(jnp.int32, (ROWS, COLS), 0)

    def interior(p, _):
        lev, f = p // FIELDS, lax.rem(p, FIELDS)
        field = comb[p]
        acc = av[lev, f] + sv[0, lev].astype(f32) * field
        acc = acc + jnp.where(row == 0, 0.0, pltpu.roll(sv[1, lev].astype(f32) * field, 1, 0))
        acc = acc + jnp.where(
            row == ROWS - 1, 0.0, pltpu.roll(sv[2, lev].astype(f32) * field, ROWS - 1, 0)
        )
        acc = acc + jnp.where(lane == 0, 0.0, pltpu.roll(sv[3, lev].astype(f32) * field, 1, 1))
        acc = acc + jnp.where(
            lane == COLS - 1, 0.0, pltpu.roll(sv[4, lev].astype(f32) * field, COLS - 1, 1)
        )
        out[lev, f] = acc
        return 0

    lax.fori_loop(0, PAIRS, interior, 0)

    for j in range(CHUNKS):

        @pl.when(y == NY - 1)
        def _(j=j):
            relay[j] = jnp.zeros((PART, COLS), f32)

        @pl.when(y == 2)
        def _(j=j):
            down(total.at[j], buf_a.at[j], j, a_sem.at[j]).wait_recv()
            relay[j] = buf_a[j]

        @pl.when(y == 1)
        def _(j=j):
            up(total.at[j], buf_b.at[j], CHUNKS + j, b_sem.at[j]).wait_recv()
            buf_b[j] = buf_a[j] + buf_b[j]

        @pl.when(y == 0)
        def _(j=j):
            down(total.at[j], buf_a.at[j], j, a_sem.at[j]).wait_recv()
            relay[j] = buf_a[j] + buf_b[j]

        higher = jnp.where(y == 1, buf_b[j], relay[j])
        below_send[j] = jnp.where(c == 1, higher + mine[j], higher)
        pltpu.make_async_remote_copy(
            src_ref=below_send.at[j], dst_ref=below.at[1, j], send_sem=below_sem.at[j],
            recv_sem=below_sem.at[CHUNKS + j], device_id=at_zc(0, 1), device_id_type=MESH,
        ).start()
        below[0, j] = jnp.where(c == 1, higher, higher + other[j])

    lane_flip = COLS - 1 - lax.broadcasted_iota(jnp.int32, (16, COLS), 1)
    for s in range(4):
        edges[s].wait()
    for s in range(2):
        strip = turned(row_got[s], seam[0, s], lane_flip)[0]
        row_got[s] = strip
        parts = turned(col_got[s], seam[0, 2 + s], lane_flip)
        for i in range(2):
            col_back[i, pl.ds(1 - s, 16, stride=2), :] = parts[i]
    col_add[0:COLS, :] = jnp.transpose(col_back[0])
    col_add[COLS:ROWS, :] = jnp.transpose(col_back[1])

    def edge_add(p, _):
        lev, f = p // FIELDS, lax.rem(p, FIELDS)
        moved = pltpu.roll(col_add[...], COLS - 1 - 2 * p, 1)
        ends = (lane == 0) | (lane == COLS - 1)
        out[lev, f] = out[lev, f] + jnp.where(ends, moved, 0.0)
        return 0

    lax.fori_loop(0, PAIRS, edge_add, 0)
    for p in range(PAIRS):
        lev, f = p // FIELDS, p % FIELDS
        out[lev, f, 0:1, :] = out[lev, f, 0:1, :] + row_got[0, p : p + 1, :]
        out[lev, f, ROWS - 1 : ROWS, :] = out[lev, f, ROWS - 1 : ROWS, :] + row_got[1, p : p + 1, :]

    for side in range(2):
        start = keep if side == 0 else give
        for j in range(CHUNKS):
            if side == 1:
                pltpu.make_async_remote_copy(
                    src_ref=below_send.at[j], dst_ref=below.at[1, j], send_sem=below_sem.at[j],
                    recv_sem=below_sem.at[CHUNKS + j], device_id=at_zc(0, 1), device_id_type=MESH,
                ).wait()
            g = (j * PART) // HALF
            at = pl.ds(pl.multiple_of(start + (j * PART) % HALF, PART), PART)
            upper = below[side, j] + comb[FIELDS + 3 * g, at, :]
            lower = upper + comb[3 * g, at, :]
            f = 1 + 3 * g
            out[1, f, at, :] = out[1, f, at, :] + wv[g, 1, at, :] * upper
            out[0, f, at, :] = out[0, f, at, :] + wv[g, 0, at, :] * lower

    pltpu.make_async_copy(got2, got2, red_send.at[1]).wait()
    for j in range(CHUNKS):

        @pl.when(y >= 1)
        def _(j=j):
            down(total.at[j], buf_a.at[j], j, a_sem.at[j]).wait_send()

        @pl.when((y == NY - 1) | (y == 0))
        def _(j=j):
            up(total.at[j], buf_b.at[j], CHUNKS + j, b_sem.at[j]).wait_send()


def per_device(krylov, adjoint, projected, stencil, column_weight, seam_turns):
    f32 = jnp.float32
    vm = pltpu.VMEM
    dma = pltpu.SemaphoreType.DMA
    anywhere = pl.BlockSpec(memory_space=pltpu.HBM)
    scalars = pl.BlockSpec(memory_space=pltpu.SMEM)
    return pl.pallas_call(
        kernel,
        out_shape=jax.ShapeDtypeStruct(adjoint.shape, f32),
        in_specs=[anywhere] * 4 + [scalars] * 2,
        out_specs=pl.BlockSpec(memory_space=pltpu.VMEM),
        scratch_shapes=[
            vm(krylov.shape, krylov.dtype), vm(adjoint.shape, f32), vm(stencil.shape, stencil.dtype),
            vm(column_weight.shape, f32), vm((PAIRS, ROWS, COLS), f32),
            vm((KRYLOV, 2, HALF, COLS), f32), vm((KRYLOV, 2, HALF, COLS), f32),
            vm((KRYLOV, 2, HALF, COLS), f32),
            vm((CHUNKS, PART, COLS), f32), vm((CHUNKS, PART, COLS), f32), vm((CHUNKS, PART, COLS), f32),
            vm((CHUNKS, PART, COLS), f32), vm((CHUNKS, PART, COLS), f32), vm((CHUNKS, PART, COLS), f32),
            vm((CHUNKS, PART, COLS), f32), vm((2, CHUNKS, PART, COLS), f32),
            vm((1, COLS), f32), vm((1, COLS), f32),
            vm((len(GROUP_XY), 1, COLS), f32), vm((len(GROUP_ZC), 1, COLS), f32),
            vm((2, 16, COLS), f32), vm((2, 16, COLS), f32), vm((ROWS, COLS), f32), vm((COLS, COLS), f32),
            vm((2, 16, ROWS), f32), vm((2, 16, ROWS), f32), vm((2, COLS, COLS), f32), vm((ROWS, COLS), f32),
            dma((2 * FIELDS + 2,)), dma((2,)), dma((2,)), dma((2,)), dma((2 * CHUNKS,)), dma((CHUNKS,)),
            dma((CHUNKS,)), dma((2 * CHUNKS,)), dma((8,)),
        ],
        name="step",
        compiler_params=pltpu.CompilerParams(
            collective_id=0, has_side_effects=True, vmem_limit_bytes=60 << 20
        ),
    )(krylov, adjoint, stencil, column_weight, projected, seam_turns)


def solution(mesh):
    placed = (
        P(None, "lev", None, "tile", None),
        P("lev", None, "tile", None),
        P(),
        P(None, "lev", "tile", None),
        P(None, "lev", "tile", None),
        P("tile", None),
    )
    return jax.shard_map(
        per_device,
        mesh=mesh,
        in_specs=placed,
        out_specs=P("lev", None, "tile", None),
        check_vma=False,
    )
```

```python
import functools

import jax
import jax.numpy as jnp
from jax import lax
from jax.experimental import pallas as pl
from jax.experimental.pallas import tpu as pltpu
from jax.sharding import PartitionSpec as P

MESH = pl.DeviceIdType.MESH
STRIDE = 4
KRYLOV = 4
FIELDS = 5
LEVELS = 2
ROWS = 256
COLS = 128
HALF = ROWS // 2
CHUNKS = 4
PART = 2 * HALF // CHUNKS
NX, NZ, NY, NC = 4, 8, 4, 2
PAIRS = LEVELS * FIELDS
COUNT = 16 * FIELDS * 8192 * COLS


def ring(d, n):
    return min(d % n, (-d) % n)


GROUP_XY = sorted(
    [(dx, dy) for dx in range(NX) for dy in range(NY) if (dx, dy) != (0, 0)],
    key=lambda o: -(ring(o[0], NX) + ring(o[1], NY)),
)
GROUP_ZC = sorted(
    [(dz, dc) for dz in range(NZ) for dc in range(NC) if (dz, dc) != (0, 0)],
    key=lambda o: -(ring(o[0], NZ) + 0.5 * o[1]),
)


def splat_sum(x):
    return jnp.sum(jnp.sum(x, axis=0, keepdims=True), axis=1, keepdims=True)


def turned(strip, turn, lane_flip):
    odd = lax.rem(turn, 2) == 1
    cosine = jnp.where(turn == 0, 1.0, jnp.where(turn == 2, -1.0, 0.0)).astype(jnp.float32)
    sine = jnp.where(turn == 1, 1.0, jnp.where(turn == 3, -1.0, 0.0)).astype(jnp.float32)
    halves = [strip[:, i : i + COLS] for i in range(0, strip.shape[1], COLS)]
    back = [jnp.take_along_axis(h, lane_flip, axis=1) for h in halves[::-1]]
    pair = lax.broadcasted_iota(jnp.int32, halves[0].shape, 0)
    field = lax.rem(pair, FIELDS)
    out = []
    for h, b in zip(halves, back):
        x = jnp.where(odd, b, h)
        after = pltpu.roll(x, x.shape[0] - 1, 0)
        before = pltpu.roll(x, 1, 0)
        out.append(
            jnp.where(
                field == 2,
                cosine * x - sine * after,
                jnp.where(field == 3, sine * before + cosine * x, x),
            )
        )
    return out


def kernel(
    k_hbm, a_hbm, s_hbm, w_hbm, p_hbm, t_hbm,
    out,
    kv, av, sv, wv, proj, seam, comb,
    ls_own, ls_send, ls_recv,
    total, mine, other, relay, buf_a, buf_b, below_send, below,
    row1, row2, got1, got2,
    row_send, row_got, col_mix, col_t, col_send, col_got, col_back, col_add,
    load_sem, red_send, red_recv, ls_sem, y_send, a_sem, b_sem, below_sem, edge_sem,
):
    t, l = lax.axis_index("tile"), lax.axis_index("lev")
    x, z, y, c = t // NZ, lax.rem(t, NZ), l // NC, lax.rem(l, NC)
    f32 = jnp.float32

    loads = []
    for f in range(FIELDS):
        loads.append(pltpu.make_async_copy(k_hbm.at[:, :, f], kv.at[:, :, f], load_sem.at[f]))
        loads.append(pltpu.make_async_copy(a_hbm.at[:, f], av.at[:, f], load_sem.at[FIELDS + f]))
    load_s = pltpu.make_async_copy(s_hbm, sv, load_sem.at[2 * FIELDS])
    load_w = pltpu.make_async_copy(w_hbm, wv, load_sem.at[2 * FIELDS + 1])
    load_p = pltpu.make_async_copy(p_hbm, proj, load_sem.at[2 * FIELDS + 2])
    load_t = pltpu.make_async_copy(t_hbm, seam, load_sem.at[2 * FIELDS + 3])
    order = [0, 3, 1, 2, 4]
    for f in order:
        loads[2 * f].start()
        loads[2 * f + 1].start()

    def at_xy(dx, dy):
        return (lax.rem(x + dx, NX) * NZ + z, lax.rem(y + dy, NY) * NC + c)

    def at_zc(dz, dc):
        return (x * NZ + lax.rem(z + dz, NZ), y * NC + lax.rem(c + dc, NC))

    def at_tile(d):
        return (lax.rem(t + d + NX * NZ, NX * NZ), l)

    peers = [at_xy(*o) for o in GROUP_XY] + [at_zc(*o) for o in GROUP_ZC]
    peers += [at_tile(d) for d in (STRIDE, -STRIDE, 1, -1)]
    barrier = pltpu.get_barrier_semaphore()
    for peer in peers:
        pl.semaphore_signal(barrier, inc=1, device_id=peer, device_id_type=MESH)
    load_s.start()
    load_w.start()
    load_p.start()
    load_t.start()

    zero8 = jnp.zeros((8, COLS), f32)
    sums = (zero8,) * KRYLOV
    keep, give = c * HALF, (1 - c) * HALF
    for f in order:
        loads[2 * f].wait()
        loads[2 * f + 1].wait()

        def dots(i, sums, f=f):
            lev, blk = i // 16, lax.rem(i, 16)
            at = pl.ds(pl.multiple_of(blk * 16, 16), 16)
            a = av[lev, f, at, :]
            out_sums = []
            for k in range(KRYLOV):
                prod = kv[k, lev, f, at, :].astype(f32) * a
                out_sums.append(sums[k] + prod[0:8] + prod[8:16])
            return tuple(out_sums)

        sums = lax.fori_loop(0, LEVELS * 16, dots, sums, unroll=4)
        if f in (0, 3):
            g = f // 3

            def level_sums(k, _, f=f, g=g):
                for dst, start in ((ls_send, give), (ls_own, keep)):
                    at = pl.ds(pl.multiple_of(start, HALF), HALF)
                    dst[k, g] = kv[k, 0, f, at, :].astype(f32) + kv[k, 1, f, at, :].astype(f32)
                return 0

            lax.fori_loop(0, KRYLOV, level_sums, 0)

    lane1 = lax.broadcasted_iota(jnp.int32, (1, COLS), 1)
    mine_row = jnp.zeros((1, COLS), f32)
    for k in range(KRYLOV):
        mine_row = jnp.where(lane1 == k, splat_sum(sums[k]), mine_row)
    row1[...] = mine_row

    pl.semaphore_wait(barrier, len(peers))

    for j, o in enumerate(GROUP_XY):
        pltpu.make_async_remote_copy(
            src_ref=row1, dst_ref=got1.at[j], send_sem=red_send.at[0], recv_sem=red_recv.at[0],
            device_id=at_xy(*o), device_id_type=MESH,
        ).start()
    swap = pltpu.make_async_remote_copy(
        src_ref=ls_send, dst_ref=ls_recv, send_sem=ls_sem.at[0], recv_sem=ls_sem.at[1],
        device_id=at_zc(0, 1), device_id_type=MESH,
    )
    swap.start()
    pltpu.make_async_copy(got1, got1, red_recv.at[0]).wait()
    stage = row1[...]
    for j in range(len(GROUP_XY)):
        stage = stage + got1[j]
    row2[...] = stage
    for j, o in enumerate(GROUP_ZC):
        pltpu.make_async_remote_copy(
            src_ref=row2, dst_ref=got2.at[j], send_sem=red_send.at[1], recv_sem=red_recv.at[1],
            device_id=at_zc(*o), device_id_type=MESH,
        ).start()
    load_s.wait()
    load_w.wait()
    load_p.wait()
    load_t.wait()
    swap.wait()
    pltpu.make_async_copy(got1, got1, red_send.at[0]).wait()
    pltpu.make_async_copy(got2, got2, red_recv.at[1]).wait()
    stage = row2[...]
    for j in range(len(GROUP_ZC)):
        stage = stage + got2[j]
    coupling = [
        jnp.sum(jnp.where(lane1 == k, stage, 0.0), axis=1, keepdims=True) * (0.5 / COUNT)
        for k in range(KRYLOV)
    ]
    mix = []
    for j in range(KRYLOV):
        m = proj[0, j] * coupling[0]
        for k in range(1, KRYLOV):
            m = m + proj[k, j] * coupling[k]
        mix.append(jnp.broadcast_to(m, (8, COLS)))

    def mixed(parts):
        acc = None
        for m, p in zip(mix, parts):
            rows = p.shape[0]
            term = jnp.concatenate([m] * (rows // 8), axis=0) * p
            acc = term if acc is None else acc + term
        return acc

    for j in range(CHUNKS):
        g, at = (j * PART) // HALF, pl.ds((j * PART) % HALF, PART)
        m = mixed([ls_own[k, g, at, :] for k in range(KRYLOV)])
        o = mixed([ls_recv[k, g, at, :] for k in range(KRYLOV)])
        mine[j] = m
        other[j] = o
        total[j] = m + o

        def down(src, dst, slot, sem):
            return pltpu.make_async_remote_copy(
                src_ref=src, dst_ref=dst, send_sem=y_send.at[slot], recv_sem=sem,
                device_id=at_xy(0, NY - 1), device_id_type=MESH,
            )

        def up(src, dst, slot, sem):
            return pltpu.make_async_remote_copy(
                src_ref=src, dst_ref=dst, send_sem=y_send.at[slot], recv_sem=sem,
                device_id=at_xy(0, 1), device_id_type=MESH,
            )

        @pl.when(y >= 2)
        def _(j=j):
            down(total.at[j], buf_a.at[j], j, a_sem.at[j]).start()

        @pl.when(y == NY - 1)
        def _(j=j):
            up(total.at[j], buf_b.at[j], CHUNKS + j, b_sem.at[j]).start()

    def combine(i, _):
        for f in range(FIELDS):
            lev, blk = i // 8, lax.rem(i, 8)
            at = pl.ds(pl.multiple_of(blk * 32, 32), 32)
            comb[lev * FIELDS + f, at, :] = mixed(
                [kv[k, lev, f, at, :].astype(f32) for k in range(KRYLOV)]
            )
        return 0

    lax.fori_loop(0, LEVELS * 8, combine, 0)

    lane = lax.broadcasted_iota(jnp.int32, (ROWS, COLS), 1)
    for p in range(PAIRS):
        lev = p // FIELDS
        row_send[0, p : p + 1, :] = (
            sv[1, lev, ROWS - 16 : ROWS, :].astype(f32)[15:16] * comb[p, ROWS - 1 : ROWS, :]
        )
        row_send[1, p : p + 1, :] = sv[2, lev, 0:16, :].astype(f32)[0:1] * comb[p, 0:1, :]

    def strips(p, _):
        lev = p // FIELDS
        field = comb[p]
        both = jnp.where(
            lane == 0, sv[4, lev].astype(f32) * field, sv[3, lev].astype(f32) * field
        )
        moved = pltpu.roll(both, 2 * p + 1, 1)
        col_mix[...] = jnp.where(lane // 2 == p, moved, col_mix[...])
        return 0

    col_mix[...] = jnp.zeros((ROWS, COLS), f32)
    row_send[:, PAIRS:, :] = jnp.zeros((2, 16 - PAIRS, COLS), f32)
    lax.fori_loop(0, PAIRS, strips, 0)
    for i in range(2):
        col_t[...] = jnp.transpose(col_mix[i * COLS : (i + 1) * COLS, :])
        for s in range(2):
            col_send[s, :, i * COLS : (i + 1) * COLS] = col_t[pl.ds(s, 16, stride=2), :]

    edges = []
    for s, (src, dst, d) in enumerate(
        (
            (row_send.at[0], row_got.at[0], 1),
            (row_send.at[1], row_got.at[1], -1),
            (col_send.at[0], col_got.at[0], STRIDE),
            (col_send.at[1], col_got.at[1], -STRIDE),
        )
    ):
        edges.append(
            pltpu.make_async_remote_copy(
                src_ref=src, dst_ref=dst, send_sem=edge_sem.at[s], recv_sem=edge_sem.at[4 + s],
                device_id=at_tile(d), device_id_type=MESH,
            )
        )
    for s in (2, 3, 0, 1):
        edges[s].start()

    for j in range(CHUNKS):

        @pl.when(y == 1)
        def _(j=j):
            down(total.at[j], buf_a.at[j], j, a_sem.at[j]).wait_recv()
            relay[j] = total[j] + buf_a[j]
            down(relay.at[j], buf_a.at[j], j, a_sem.at[j]).start()

        @pl.when(y == 0)
        def _(j=j):
            up(total.at[j], buf_b.at[j], CHUNKS + j, b_sem.at[j]).wait_recv()
            up(buf_b.at[j], buf_b.at[j], CHUNKS + j, b_sem.at[j]).start()

    row = lax.broadcasted_iota(jnp.int32, (ROWS, COLS), 0)

    def interior(p, _):
        lev, f = p // FIELDS, lax.rem(p, FIELDS)
        field = comb[p]
        acc = av[lev, f] + sv[0, lev].astype(f32) * field
        acc = acc + jnp.where(row == 0, 0.0, pltpu.roll(sv[1, lev].astype(f32) * field, 1, 0))
        acc = acc + jnp.where(
            row == ROWS - 1, 0.0, pltpu.roll(sv[2, lev].astype(f32) * field, ROWS - 1, 0)
        )
        acc = acc + jnp.where(lane == 0, 0.0, pltpu.roll(sv[3, lev].astype(f32) * field, 1, 1))
        acc = acc + jnp.where(
            lane == COLS - 1, 0.0, pltpu.roll(sv[4, lev].astype(f32) * field, COLS - 1, 1)
        )
        out[lev, f] = acc
        return 0

    lax.fori_loop(0, PAIRS, interior, 0)

    for j in range(CHUNKS):

        @pl.when(y == NY - 1)
        def _(j=j):
            relay[j] = jnp.zeros((PART, COLS), f32)

        @pl.when(y == 2)
        def _(j=j):
            down(total.at[j], buf_a.at[j], j, a_sem.at[j]).wait_recv()
            relay[j] = buf_a[j]

        @pl.when(y == 1)
        def _(j=j):
            up(total.at[j], buf_b.at[j], CHUNKS + j, b_sem.at[j]).wait_recv()
            buf_b[j] = buf_a[j] + buf_b[j]

        @pl.when(y == 0)
        def _(j=j):
            down(total.at[j], buf_a.at[j], j, a_sem.at[j]).wait_recv()
            relay[j] = buf_a[j] + buf_b[j]

        higher = jnp.where(y == 1, buf_b[j], relay[j])
        below_send[j] = jnp.where(c == 1, higher + mine[j], higher)
        pltpu.make_async_remote_copy(
            src_ref=below_send.at[j], dst_ref=below.at[1, j], send_sem=below_sem.at[j],
            recv_sem=below_sem.at[CHUNKS + j], device_id=at_zc(0, 1), device_id_type=MESH,
        ).start()
        below[0, j] = jnp.where(c == 1, higher, higher + other[j])

    lane_flip = COLS - 1 - lax.broadcasted_iota(jnp.int32, (16, COLS), 1)
    for s in range(4):
        edges[s].wait()
    for s in range(2):
        strip = turned(row_got[s], seam[0, s], lane_flip)[0]
        row_got[s] = strip
        parts = turned(col_got[s], seam[0, 2 + s], lane_flip)
        for i in range(2):
            col_back[i, pl.ds(1 - s, 16, stride=2), :] = parts[i]
    col_add[0:COLS, :] = jnp.transpose(col_back[0])
    col_add[COLS:ROWS, :] = jnp.transpose(col_back[1])

    def edge_add(p, _):
        lev, f = p // FIELDS, lax.rem(p, FIELDS)
        moved = pltpu.roll(col_add[...], COLS - 1 - 2 * p, 1)
        ends = (lane == 0) | (lane == COLS - 1)
        out[lev, f] = out[lev, f] + jnp.where(ends, moved, 0.0)
        return 0

    lax.fori_loop(0, PAIRS, edge_add, 0)
    for p in range(PAIRS):
        lev, f = p // FIELDS, p % FIELDS
        out[lev, f, 0:1, :] = out[lev, f, 0:1, :] + row_got[0, p : p + 1, :]
        out[lev, f, ROWS - 1 : ROWS, :] = out[lev, f, ROWS - 1 : ROWS, :] + row_got[1, p : p + 1, :]

    for side in range(2):
        start = keep if side == 0 else give
        for j in range(CHUNKS):
            if side == 1:
                pltpu.make_async_remote_copy(
                    src_ref=below_send.at[j], dst_ref=below.at[1, j], send_sem=below_sem.at[j],
                    recv_sem=below_sem.at[CHUNKS + j], device_id=at_zc(0, 1), device_id_type=MESH,
                ).wait()
            g = (j * PART) // HALF
            at = pl.ds(pl.multiple_of(start + (j * PART) % HALF, PART), PART)
            upper = below[side, j] + comb[FIELDS + 3 * g, at, :]
            lower = upper + comb[3 * g, at, :]
            f = 1 + 3 * g
            out[1, f, at, :] = out[1, f, at, :] + wv[g, 1, at, :] * upper
            out[0, f, at, :] = out[0, f, at, :] + wv[g, 0, at, :] * lower

    pltpu.make_async_copy(got2, got2, red_send.at[1]).wait()
    for j in range(CHUNKS):

        @pl.when(y >= 1)
        def _(j=j):
            down(total.at[j], buf_a.at[j], j, a_sem.at[j]).wait_send()

        @pl.when((y == NY - 1) | (y == 0))
        def _(j=j):
            up(total.at[j], buf_b.at[j], CHUNKS + j, b_sem.at[j]).wait_send()


def per_device(krylov, adjoint, projected, stencil, column_weight, seam_turns):
    f32 = jnp.float32
    vm = pltpu.VMEM
    dma = pltpu.SemaphoreType.DMA
    anywhere = pl.BlockSpec(memory_space=pltpu.HBM)
    return pl.pallas_call(
        kernel,
        out_shape=jax.ShapeDtypeStruct(adjoint.shape, f32),
        in_specs=[anywhere] * 6,
        out_specs=pl.BlockSpec(memory_space=pltpu.VMEM),
        scratch_shapes=[
            vm(krylov.shape, krylov.dtype), vm(adjoint.shape, f32), vm(stencil.shape, stencil.dtype),
            vm(column_weight.shape, f32),
            pltpu.SMEM(projected.shape, f32), pltpu.SMEM(seam_turns.shape, jnp.int32),
            vm((PAIRS, ROWS, COLS), f32),
            vm((KRYLOV, 2, HALF, COLS), f32), vm((KRYLOV, 2, HALF, COLS), f32),
            vm((KRYLOV, 2, HALF, COLS), f32),
            vm((CHUNKS, PART, COLS), f32), vm((CHUNKS, PART, COLS), f32), vm((CHUNKS, PART, COLS), f32),
            vm((CHUNKS, PART, COLS), f32), vm((CHUNKS, PART, COLS), f32), vm((CHUNKS, PART, COLS), f32),
            vm((CHUNKS, PART, COLS), f32), vm((2, CHUNKS, PART, COLS), f32),
            vm((1, COLS), f32), vm((1, COLS), f32),
            vm((len(GROUP_XY), 1, COLS), f32), vm((len(GROUP_ZC), 1, COLS), f32),
            vm((2, 16, COLS), f32), vm((2, 16, COLS), f32), vm((ROWS, COLS), f32), vm((COLS, COLS), f32),
            vm((2, 16, ROWS), f32), vm((2, 16, ROWS), f32), vm((2, COLS, COLS), f32), vm((ROWS, COLS), f32),
            dma((2 * FIELDS + 4,)), dma((2,)), dma((2,)), dma((2,)), dma((2 * CHUNKS,)), dma((CHUNKS,)),
            dma((CHUNKS,)), dma((2 * CHUNKS,)), dma((8,)),
        ],
        name="step",
        compiler_params=pltpu.CompilerParams(
            collective_id=0, has_side_effects=True, vmem_limit_bytes=24 << 20
        ),
    )(
        *[
            pltpu.with_memory_space_constraint(a, pltpu.HBM)
            for a in (krylov, adjoint, stencil, column_weight, projected, seam_turns)
        ]
    )


def solution(mesh):
    placed = (
        P(None, "lev", None, "tile", None),
        P("lev", None, "tile", None),
        P(),
        P(None, "lev", "tile", None),
        P(None, "lev", "tile", None),
        P("tile", None),
    )
    return jax.shard_map(
        per_device,
        mesh=mesh,
        in_specs=placed,
        out_specs=P("lev", None, "tile", None),
        check_vma=False,
    )
```

```python
import jax
import jax.numpy as jnp
from jax import lax
from jax.experimental import pallas as pl
from jax.experimental.pallas import tpu as pltpu
from jax.sharding import PartitionSpec as P

MESH = pl.DeviceIdType.MESH
STRIDE = 4
KRYLOV = 4
FIELDS = 5
LEVELS = 2
ROWS = 256
COLS = 128
HALF = ROWS // 2
NX, NZ, NY, NC = 4, 8, 4, 2
PAIRS = LEVELS * FIELDS
STRIPS = KRYLOV * PAIRS
CHUNKS = 8
PART = 2 * HALF // CHUNKS
DIRECT = 2
RELAYED = CHUNKS - DIRECT
COUNT = 16 * FIELDS * 8192 * COLS


def ring(d, n):
    return min(d % n, (-d) % n)


GROUP_XY = sorted(
    [(dx, dy) for dx in range(NX) for dy in range(NY) if (dx, dy) != (0, 0)],
    key=lambda o: -(ring(o[0], NX) + ring(o[1], NY)),
)
GROUP_ZC = sorted(
    [(dz, dc) for dz in range(NZ) for dc in range(NC) if (dz, dc) != (0, 0)],
    key=lambda o: -(ring(o[0], NZ) + 0.5 * o[1]),
)


def splat_sum(x):
    return jnp.sum(jnp.sum(x, axis=0, keepdims=True), axis=1, keepdims=True)


def turned(strip, turn, lane_flip):
    odd = lax.rem(turn, 2) == 1
    cosine = jnp.where(turn == 0, 1.0, jnp.where(turn == 2, -1.0, 0.0)).astype(jnp.float32)
    sine = jnp.where(turn == 1, 1.0, jnp.where(turn == 3, -1.0, 0.0)).astype(jnp.float32)
    halves = [strip[:, i : i + COLS] for i in range(0, strip.shape[1], COLS)]
    back = [jnp.take_along_axis(h, lane_flip, axis=1) for h in halves[::-1]]
    field = lax.rem(lax.broadcasted_iota(jnp.int32, halves[0].shape, 0), FIELDS)
    out = []
    for h, b in zip(halves, back):
        x = jnp.where(odd, b, h)
        after = pltpu.roll(x, x.shape[0] - 1, 0)
        before = pltpu.roll(x, 1, 0)
        out.append(
            jnp.where(
                field == 2,
                cosine * x - sine * after,
                jnp.where(field == 3, sine * before + cosine * x, x),
            )
        )
    return out


def kernel(
    k_hbm, a_hbm, s_hbm, w_hbm, p_hbm, t_hbm,
    out,
    kv, av, sv, wv, proj, seam, coef, comb, pick, pick_coef,
    ls_own, ls_send, ls_recv, total, mine, relay, buf_a, buf_b, buf_c, below_send, below,
    row1, row2, got1, got2,
    row_send, row_got, row_mix, col_mix, col_t, col_send, col_got, strip_mix, col_back, col_add,
    load_sem, red_send, red_recv, swap_sem, y_send, a_sem, b_sem, c_sem, below_sem, edge_sem,
):
    t, l = lax.axis_index("tile"), lax.axis_index("lev")
    x, z, y, c = t // NZ, lax.rem(t, NZ), l // NC, lax.rem(l, NC)
    f32 = jnp.float32

    load_k = [pltpu.make_async_copy(k_hbm.at[:, :, f], kv.at[:, :, f], load_sem.at[f]) for f in range(FIELDS)]
    load_a = [pltpu.make_async_copy(a_hbm.at[:, f], av.at[:, f], load_sem.at[FIELDS + f]) for f in range(FIELDS)]
    load_s = pltpu.make_async_copy(s_hbm, sv, load_sem.at[2 * FIELDS])
    load_w = pltpu.make_async_copy(w_hbm, wv, load_sem.at[2 * FIELDS + 1])
    load_p = pltpu.make_async_copy(p_hbm, proj, load_sem.at[2 * FIELDS + 2])
    load_t = pltpu.make_async_copy(t_hbm, seam, load_sem.at[2 * FIELDS + 3])
    for f in range(FIELDS):
        load_k[f].start()
        load_a[f].start()

    def at_xy(dx, dy):
        return (lax.rem(x + dx, NX) * NZ + z, lax.rem(y + dy, NY) * NC + c)

    def at_zc(dz, dc):
        return (x * NZ + lax.rem(z + dz, NZ), y * NC + lax.rem(c + dc, NC))

    def at_tile(d):
        return (lax.rem(t + d + NX * NZ, NX * NZ), l)

    def remote(src, dst, send, recv, device):
        return pltpu.make_async_remote_copy(
            src_ref=src, dst_ref=dst, send_sem=send, recv_sem=recv, device_id=device, device_id_type=MESH
        )

    xy, zc = [at_xy(*o) for o in GROUP_XY], [at_zc(*o) for o in GROUP_ZC]
    core_peer, below_peer, above_peer = at_zc(0, 1), at_xy(0, NY - 1), at_xy(0, 1)
    edge_peers = [at_tile(d) for d in (1, -1, STRIDE, -STRIDE)]
    peers = edge_peers + xy + zc
    barrier = pltpu.get_barrier_semaphore()
    for peer in peers:
        pl.semaphore_signal(barrier, inc=1, device_id=peer, device_id_type=MESH)
    for load in (load_s, load_w, load_p, load_t):
        load.start()

    li = lax.broadcasted_iota(jnp.int32, (COLS, COLS), 0)
    lj = lax.broadcasted_iota(jnp.int32, (COLS, COLS), 1)

    def store_mask(ref, i, mask):
        ref[i] = jnp.where(mask, 1.0, 0.0).astype(jnp.bfloat16)

    for p in range(PAIRS):
        store_mask(pick, p, ((li == COLS - 1) & (lj == 2 * p)) | ((li == 0) & (lj == 2 * p + 1)))
    pair = lax.rem(lj, 2 * PAIRS)
    for lev in range(LEVELS):
        here = (pair >= 2 * FIELDS * lev) & (pair < 2 * FIELDS * (lev + 1)) & (lj < 2 * STRIPS)
        store_mask(pick_coef, lev, here & (li == COLS - 1) & (lax.rem(lj, 2) == 0))
        store_mask(pick_coef, LEVELS + lev, here & (li == 0) & (lax.rem(lj, 2) == 1))

    sums = (jnp.zeros((16, COLS), f32),) * KRYLOV
    for f in range(FIELDS):
        load_k[f].wait()
        load_a[f].wait()

        def dots(i, sums, f=f):
            lev, blk = i // 16, lax.rem(i, 16)
            at = pl.ds(pl.multiple_of(blk * 16, 16), 16)
            a = av[lev, f, at, :]
            return tuple(sums[k] + kv[k, lev, f, at, :].astype(f32) * a for k in range(KRYLOV))

        sums = lax.fori_loop(0, LEVELS * 16, dots, sums, unroll=4)

    lane1 = lax.broadcasted_iota(jnp.int32, (1, COLS), 1)
    mine_row = jnp.zeros((1, COLS), f32)
    for k in range(KRYLOV):
        mine_row = jnp.where(lane1 == k, splat_sum(sums[k]), mine_row)
    row1[...] = mine_row

    pl.semaphore_wait(barrier, len(peers))

    for j in range(len(xy)):
        remote(row1, got1.at[j], red_send.at[0], red_recv.at[0], xy[j]).start()

    keep, give = c * HALF, (1 - c) * HALF

    def swap(k):
        return remote(ls_send.at[k], ls_recv.at[k], swap_sem.at[0, k], swap_sem.at[1, k], core_peer)

    def level_sums(k, _):
        for g in range(2):
            for dst, start in ((ls_send, give), (ls_own, keep)):
                at = pl.ds(pl.multiple_of(start, HALF), HALF)
                dst[k, g] = kv[k, 0, 3 * g, at, :].astype(f32) + kv[k, 1, 3 * g, at, :].astype(f32)
        swap(k).start()
        return 0

    lax.fori_loop(0, KRYLOV, level_sums, 0)

    load_s.wait()
    parts = [sv[3, 0], sv[3, 1], sv[4, 0], sv[4, 1]]
    at_ends = sum(jnp.dot(parts[i], pick_coef[i], preferred_element_type=f32) for i in range(4))
    mixed = None
    for k in range(KRYLOV):
        strips = sum(
            jnp.dot(kv[k, p // FIELDS, p % FIELDS], pick[p], preferred_element_type=f32) for p in range(PAIRS)
        )
        strips = pltpu.roll(strips, 2 * PAIRS * k, 1) if k else strips
        mixed = strips if mixed is None else mixed + strips
    col_mix[...] = mixed * at_ends

    def edge_rows(k, _):
        for p in range(PAIRS):
            lev, f = p // FIELDS, p % FIELDS
            last = sv[1, lev, ROWS - 16 : ROWS, :].astype(f32) * kv[k, lev, f, ROWS - 16 : ROWS, :].astype(f32)
            first = sv[2, lev, 0:16, :].astype(f32) * kv[k, lev, f, 0:16, :].astype(f32)
            row_send[0, pl.ds(k * PAIRS + p, 1), :] = last[15:16]
            row_send[1, pl.ds(k * PAIRS + p, 1), :] = first[0:1]
        return 0

    lax.fori_loop(0, KRYLOV, edge_rows, 0)
    for i in range(2):
        col_t[...] = jnp.transpose(col_mix[i * COLS : (i + 1) * COLS, :])
        for s in range(2):
            col_send[s, :, i * COLS : (i + 1) * COLS] = col_t[pl.ds(s, STRIPS, stride=2), :]

    lane = lax.broadcasted_iota(jnp.int32, (ROWS, COLS), 1)
    row = lax.broadcasted_iota(jnp.int32, (ROWS, COLS), 0)
    for lev in range(LEVELS):
        coef[0, lev] = sv[0, lev].astype(f32)
        coef[1, lev] = jnp.where(row == ROWS - 1, 0.0, sv[1, lev].astype(f32))
        coef[2, lev] = jnp.where(row == 0, 0.0, sv[2, lev].astype(f32))
        coef[3, lev] = jnp.where(lane == COLS - 1, 0.0, sv[3, lev].astype(f32))
        coef[4, lev] = jnp.where(lane == 0, 0.0, sv[4, lev].astype(f32))

    pltpu.make_async_copy(got1, got1, red_recv.at[0]).wait()
    stage = row1[...]
    for j in range(len(xy)):
        stage = stage + got1[j]
    row2[...] = stage
    for j in range(len(zc)):
        remote(row2, got2.at[j], red_send.at[1], red_recv.at[1], zc[j]).start()

    edges = [
        remote(src, dst, edge_sem.at[s], edge_sem.at[4 + s], edge_peers[s])
        for s, (src, dst) in enumerate(
            (
                (row_send.at[0], row_got.at[0]),
                (row_send.at[1], row_got.at[1]),
                (col_send.at[0], col_got.at[0]),
                (col_send.at[1], col_got.at[1]),
            )
        )
    ]
    for s in (2, 3, 0, 1):
        edges[s].start()

    for k in range(KRYLOV):
        swap(k).wait()
        ls_send[k] = ls_own[k] + ls_recv[k]
    for load in (load_w, load_p, load_t):
        load.wait()
    pltpu.make_async_copy(got1, got1, red_send.at[0]).wait()

    pltpu.make_async_copy(got2, got2, red_recv.at[1]).wait()
    stage = row2[...]
    for j in range(len(zc)):
        stage = stage + got2[j]
    coupling = [
        jnp.sum(jnp.where(lane1 == k, stage, 0.0), axis=1, keepdims=True) * (0.5 / COUNT)
        for k in range(KRYLOV)
    ]
    mix, mix_one = [], []
    for j in range(KRYLOV):
        m = proj[0, j] * coupling[0]
        for k in range(1, KRYLOV):
            m = m + proj[k, j] * coupling[k]
        mix_one.append(m)
        mix.append(jnp.broadcast_to(m, (8, COLS)))

    def mixed(parts):
        acc = None
        for m, p in zip(mix, parts):
            term = jnp.concatenate([m] * (p.shape[0] // 8), axis=0) * p
            acc = term if acc is None else acc + term
        return acc

    def down(src, j):
        return remote(src.at[j], buf_a.at[j], y_send.at[0, j], a_sem.at[j], below_peer)

    def up(src, j):
        return remote(src.at[j], buf_b.at[j], y_send.at[1, j], b_sem.at[j], above_peer)

    def two_down(j):
        return remote(total.at[j], buf_c.at[j - RELAYED], y_send.at[2, j], c_sem.at[j - RELAYED], at_xy(0, 2))

    def two_up(j):
        return remote(total.at[j], buf_b.at[j], y_send.at[2, j], b_sem.at[j], at_xy(0, 2))

    for j in range(CHUNKS):
        g, at = (j * PART) // HALF, pl.ds((j * PART) % HALF, PART)
        total[j] = mixed([ls_send[k, g, at, :] for k in range(KRYLOV)])

        @pl.when(y == NY - 1)
        def _(j=j):
            if j >= RELAYED:
                two_up(j).start()
            down(total, j).start()
            up(total, j).start()

        @pl.when(y == 2)
        def _(j=j):
            if j >= RELAYED:
                two_down(j).start()
            down(total, j).start()

        if j >= RELAYED:

            @pl.when(y == 1)
            def _(j=j):
                down(total, j).start()

    for j in range(CHUNKS):
        g, at = (j * PART) // HALF, pl.ds((j * PART) % HALF, PART)
        mine[j] = mixed([ls_own[k, g, at, :] for k in range(KRYLOV)])

    @pl.when(y == NY - 1)
    def _():
        buf_a[...] = jnp.zeros(buf_a.shape, f32)

    @pl.when(y >= 2)
    def _():
        buf_b[...] = jnp.zeros(buf_b.shape, f32)

    @pl.when(y >= 1)
    def _():
        buf_c[...] = jnp.zeros(buf_c.shape, f32)

    def combine(i, _):
        lev, blk = i // 8, lax.rem(i, 8)
        at = pl.ds(pl.multiple_of(blk * 32, 32), 32)
        for f in range(FIELDS):
            comb[lev * FIELDS + f, at, :] = mixed([kv[k, lev, f, at, :].astype(f32) for k in range(KRYLOV)])
        return 0

    lax.fori_loop(0, LEVELS * 8, combine, 0)

    outer = (lane == 0) | (lane == COLS - 1)

    def interior(p, _):
        lev, f = p // FIELDS, lax.rem(p, FIELDS)
        field = comb[p]
        acc = av[lev, f] + jnp.where(outer, pltpu.roll(col_add[...], COLS - 1 - 2 * p, 1), 0.0)
        acc = acc + coef[0, lev] * field
        acc = acc + pltpu.roll(coef[1, lev] * field, 1, 0)
        acc = acc + pltpu.roll(coef[2, lev] * field, ROWS - 1, 0)
        acc = acc + pltpu.roll(coef[3, lev] * field, 1, 1)
        acc = acc + pltpu.roll(coef[4, lev] * field, COLS - 1, 1)
        out[lev, f] = acc
        out[lev, f, 0:1, :] = acc[0:1] + row_mix[0, pl.ds(p, 1), :]
        out[lev, f, ROWS - 1 : ROWS, :] = acc[ROWS - 1 : ROWS] + row_mix[1, pl.ds(p, 1), :]
        return 0

    def pass_on(j, _):
        @pl.when(y == 1)
        def _():
            down(total, j).wait_recv()
            relay[j] = total[j] + buf_a[j]
            down(relay, j).start()

        @pl.when(y == 0)
        def _():
            up(total, j).wait_recv()
            up(buf_b, j).start()

        return 0

    lax.fori_loop(0, RELAYED // 2, pass_on, 0)

    for s in range(4):
        edges[s].wait()

    def mixed_strips(ref, s):
        return sum(mix_one[k] * ref[s, k * PAIRS : (k + 1) * PAIRS, :] for k in range(KRYLOV))

    lane_flip = COLS - 1 - lax.broadcasted_iota(jnp.int32, (16, COLS), 1)
    for s in range(2):
        row_mix[s, 0:PAIRS, :] = mixed_strips(row_got, s)
        strip_mix[s, 0:PAIRS, :] = mixed_strips(col_got, s)
    for s in range(2):
        row_mix[s] = turned(row_mix[s], seam[0, s], lane_flip)[0]
        parts = turned(strip_mix[s], seam[0, 2 + s], lane_flip)
        for i in range(2):
            col_back[i, pl.ds(1 - s, 16, stride=2), :] = parts[i]
    col_add[0:COLS, :] = jnp.transpose(col_back[0])
    col_add[COLS:ROWS, :] = jnp.transpose(col_back[1])

    def pass_and_interior(j, _):
        pass_on(RELAYED // 2 + j, 0)
        steps = RELAYED - RELAYED // 2
        lax.fori_loop(j * PAIRS // steps, (j + 1) * PAIRS // steps, interior, 0)
        return 0

    lax.fori_loop(0, RELAYED - RELAYED // 2, pass_and_interior, 0)

    def hand(j):
        return remote(below_send.at[j], below.at[j], below_sem.at[0, j], below_sem.at[1, j], core_peer)

    def integrals(j, start, sums):
        g = (j * PART) // HALF
        at = pl.ds(pl.multiple_of(start + lax.rem(j * PART, HALF), PART), PART)
        upper = sums + comb[FIELDS + 3 * g, at, :]
        lower = upper + comb[3 * g, at, :]
        f = 1 + 3 * g
        out[1, f, at, :] = out[1, f, at, :] + wv[g, 1, at, :] * upper
        out[0, f, at, :] = out[0, f, at, :] + wv[g, 0, at, :] * lower

    def finish_mine(j, _, direct=False):
        @pl.when((y == 2) | (y == 0))
        def _():
            down(total, j).wait_recv()

        @pl.when(y == 1)
        def _():
            up(total, j).wait_recv()
            if direct:
                down(total, j).wait_recv()

        if direct:

            @pl.when(y == 0)
            def _():
                up(total, j).wait_recv()
                two_down(j).wait_recv()

        higher = buf_a[j] + buf_b[j]
        if direct:
            higher = higher + buf_c[j - RELAYED]
        below_send[j] = jnp.where(c == 1, higher + mine[j], higher)
        hand(j).start()
        integrals(j, keep, jnp.where(c == 1, higher, higher + (total[j] - mine[j])))
        return 0

    def finish_other(j, _):
        hand(j).wait()
        integrals(j, give, below[j])
        return 0

    lax.fori_loop(0, RELAYED, finish_mine, 0)
    lax.fori_loop(RELAYED, CHUNKS, lambda j, _: finish_mine(j, 0, True), 0)

    def sent(j, _, direct=False):
        @pl.when(y >= 1)
        def _():
            down(total, j).wait_send()

        @pl.when((y == NY - 1) if direct else ((y == NY - 1) | (y == 0)))
        def _():
            up(total, j).wait_send()

        if direct:

            @pl.when(y >= 2)
            def _():
                two_down(j).wait_send()

        return 0

    lax.fori_loop(0, RELAYED, sent, 0)
    lax.fori_loop(RELAYED, CHUNKS, lambda j, _: sent(j, 0, True), 0)
    pltpu.make_async_copy(got2, got2, red_send.at[1]).wait()
    lax.fori_loop(0, CHUNKS, finish_other, 0)


def per_device(krylov, adjoint, projected, stencil, column_weight, seam_turns):
    f32 = jnp.float32
    vm = pltpu.VMEM
    dma = pltpu.SemaphoreType.DMA
    part = vm((CHUNKS, PART, COLS), f32)
    sums = vm((KRYLOV, 2, HALF, COLS), f32)
    return pl.pallas_call(
        kernel,
        out_shape=jax.ShapeDtypeStruct(adjoint.shape, f32),
        in_specs=[pl.BlockSpec(memory_space=pltpu.HBM)] * 6,
        out_specs=pl.BlockSpec(memory_space=pltpu.VMEM),
        scratch_shapes=[
            vm(krylov.shape, krylov.dtype), vm(adjoint.shape, f32), vm(stencil.shape, stencil.dtype),
            vm(column_weight.shape, f32),
            pltpu.SMEM(projected.shape, f32), pltpu.SMEM(seam_turns.shape, jnp.int32),
            vm(stencil.shape, f32), vm((PAIRS, ROWS, COLS), f32),
            vm((PAIRS, COLS, COLS), jnp.bfloat16), vm((2 * LEVELS, COLS, COLS), jnp.bfloat16),
            sums, sums, sums, part, part, part, part, part, vm((max(DIRECT, 1), PART, COLS), f32), part, part,
            vm((1, COLS), f32), vm((1, COLS), f32),
            vm((len(GROUP_XY), 1, COLS), f32), vm((len(GROUP_ZC), 1, COLS), f32),
            vm((2, STRIPS, COLS), f32), vm((2, STRIPS, COLS), f32), vm((2, 16, COLS), f32), vm((ROWS, COLS), f32),
            vm((COLS, COLS), f32), vm((2, STRIPS, ROWS), f32), vm((2, STRIPS, ROWS), f32), vm((2, 16, ROWS), f32),
            vm((2, COLS, COLS), f32), vm((ROWS, COLS), f32),
            dma((2 * FIELDS + 4,)), dma((2,)), dma((2,)), dma((2, KRYLOV)), dma((3, CHUNKS)), dma((CHUNKS,)),
            dma((CHUNKS,)), dma((max(DIRECT, 1),)), dma((2, CHUNKS)), dma((8,)),
        ],
        name="step",
        compiler_params=pltpu.CompilerParams(
            collective_id=0, has_side_effects=True, vmem_limit_bytes=32 << 20
        ),
    )(
        *[
            pltpu.with_memory_space_constraint(a, pltpu.HBM)
            for a in (krylov, adjoint, stencil, column_weight, projected, seam_turns)
        ]
    )


def solution(mesh):
    placed = (
        P(None, "lev", None, "tile", None),
        P("lev", None, "tile", None),
        P(),
        P(None, "lev", "tile", None),
        P(None, "lev", "tile", None),
        P("tile", None),
    )
    return jax.shard_map(
        per_device,
        mesh=mesh,
        in_specs=placed,
        out_specs=P("lev", None, "tile", None),
        check_vma=False,
    )
```

```python
import jax
import jax.numpy as jnp
from jax import lax
from jax.experimental import pallas as pl
from jax.experimental.pallas import tpu as pltpu
from jax.sharding import PartitionSpec as P

MESH = pl.DeviceIdType.MESH
STRIDE = 4
KRYLOV = 4
FIELDS = 5
LEVELS = 2
ROWS = 256
COLS = 128
HALF = ROWS // 2
NX, NZ, NY, NC = 4, 8, 4, 2
PAIRS = LEVELS * FIELDS
STRIPS = KRYLOV * PAIRS
CHUNKS = 8
PART = 2 * HALF // CHUNKS
EARLY = 4
EARLIEST = 1
COUNT = 16 * FIELDS * 8192 * COLS


def ring(d, n):
    return min(d % n, (-d) % n)


def group(nx, nz, ny, nc):
    offsets = [
        (dx, dz, dy, dc) for dx in range(nx) for dz in range(nz) for dy in range(ny) for dc in range(nc)
    ]
    return sorted(
        offsets[1:], key=lambda o: -(ring(o[0], NX) + ring(o[1], NZ) + ring(o[2], NY) + 0.5 * o[3])
    )


FIRST = group(NX, 1, NY, 1)
SECOND = group(1, NZ, 1, NC)
UNROLL = 16


def splat_sum(x):
    return jnp.sum(jnp.sum(x, axis=0, keepdims=True), axis=1, keepdims=True)


def turned(strip, turn, lane_flip):
    odd = lax.rem(turn, 2) == 1
    cosine = jnp.where(turn == 0, 1.0, jnp.where(turn == 2, -1.0, 0.0)).astype(jnp.float32)
    sine = jnp.where(turn == 1, 1.0, jnp.where(turn == 3, -1.0, 0.0)).astype(jnp.float32)
    halves = [strip[:, i : i + COLS] for i in range(0, strip.shape[1], COLS)]
    back = [jnp.take_along_axis(h, lane_flip, axis=1) for h in halves[::-1]]
    field = lax.rem(lax.broadcasted_iota(jnp.int32, halves[0].shape, 0), FIELDS)
    out = []
    for h, b in zip(halves, back):
        x = jnp.where(odd, b, h)
        after = pltpu.roll(x, x.shape[0] - 1, 0)
        before = pltpu.roll(x, 1, 0)
        out.append(
            jnp.where(
                field == 2,
                cosine * x - sine * after,
                jnp.where(field == 3, sine * before + cosine * x, x),
            )
        )
    return out


def kernel(
    k_hbm, a_hbm, s_hbm, w_hbm, p_hbm, t_hbm,
    out,
    kv, av, sv, wv, proj, seam, coef, comb, pick, pick_coef,
    ls_own, ls_send, ls_recv, total, mine, relay, buf_a, buf_b, raw_a, raw_b, below_send, below,
    row1, row2, got1, got2,
    row_send, row_got, row_mix, col_mix, col_t, col_send, col_got, strip_mix, col_back, col_add,
    load_sem, red_send, red_recv, swap_sem, y_send, a_sem, b_sem, raw_send, raw_a_sem, raw_b_sem, below_sem, edge_sem,
):
    t, l = lax.axis_index("tile"), lax.axis_index("lev")
    x, z, y, c = t // NZ, lax.rem(t, NZ), l // NC, lax.rem(l, NC)
    f32 = jnp.float32

    load_k = [pltpu.make_async_copy(k_hbm.at[:, :, f], kv.at[:, :, f], load_sem.at[f]) for f in range(FIELDS)]
    load_a = [pltpu.make_async_copy(a_hbm.at[:, f], av.at[:, f], load_sem.at[FIELDS + f]) for f in range(FIELDS)]
    load_s = pltpu.make_async_copy(s_hbm, sv, load_sem.at[2 * FIELDS])
    load_w = pltpu.make_async_copy(w_hbm, wv, load_sem.at[2 * FIELDS + 1])
    load_p = pltpu.make_async_copy(p_hbm, proj, load_sem.at[2 * FIELDS + 2])
    load_t = pltpu.make_async_copy(t_hbm, seam, load_sem.at[2 * FIELDS + 3])
    for f in range(FIELDS):
        load_k[f].start()
        load_a[f].start()

    def device(dx, dz, dy, dc):
        return (
            lax.rem(x + dx, NX) * NZ + lax.rem(z + dz, NZ), lax.rem(y + dy, NY) * NC + lax.rem(c + dc, NC)
        )

    def at_tile(d):
        return (lax.rem(t + d + NX * NZ, NX * NZ), l)

    def remote(src, dst, send, recv, where):
        return pltpu.make_async_remote_copy(
            src_ref=src, dst_ref=dst, send_sem=send, recv_sem=recv, device_id=where, device_id_type=MESH
        )

    first, second = [device(*o) for o in FIRST], [device(*o) for o in SECOND]
    core_peer, below_peer, above_peer = device(0, 0, 0, 1), device(0, 0, NY - 1, 0), device(0, 0, 1, 0)
    edge_peers = [at_tile(d) for d in (1, -1, STRIDE, -STRIDE)]
    peers = edge_peers + first + second
    barrier = pltpu.get_barrier_semaphore()
    for peer in peers:
        pl.semaphore_signal(barrier, inc=1, device_id=peer, device_id_type=MESH)
    for load in (load_s, load_w, load_p, load_t):
        load.start()

    li = lax.broadcasted_iota(jnp.int32, (COLS, COLS), 0)
    lj = lax.broadcasted_iota(jnp.int32, (COLS, COLS), 1)

    def store_mask(ref, i, mask):
        ref[i] = jnp.where(mask, 1.0, 0.0).astype(jnp.bfloat16)

    for p in range(PAIRS):
        store_mask(pick, p, ((li == COLS - 1) & (lj == 2 * p)) | ((li == 0) & (lj == 2 * p + 1)))
    pair = lax.rem(lj, 2 * PAIRS)
    for lev in range(LEVELS):
        here = (pair >= 2 * FIELDS * lev) & (pair < 2 * FIELDS * (lev + 1)) & (lj < 2 * STRIPS)
        store_mask(pick_coef, lev, here & (li == COLS - 1) & (lax.rem(lj, 2) == 0))
        store_mask(pick_coef, LEVELS + lev, here & (li == 0) & (lax.rem(lj, 2) == 1))

    sums = (jnp.zeros((16, COLS), f32),) * KRYLOV
    for f in range(FIELDS):
        load_k[f].wait()
        load_a[f].wait()

        def dots(i, sums, f=f):
            lev, blk = i // 16, lax.rem(i, 16)
            at = pl.ds(pl.multiple_of(blk * 16, 16), 16)
            a = av[lev, f, at, :]
            return tuple(sums[k] + kv[k, lev, f, at, :].astype(f32) * a for k in range(KRYLOV))

        sums = lax.fori_loop(0, LEVELS * 16, dots, sums, unroll=UNROLL)

    lane1 = lax.broadcasted_iota(jnp.int32, (1, COLS), 1)
    mine_row = jnp.zeros((1, COLS), f32)
    for k in range(KRYLOV):
        mine_row = jnp.where(lane1 == k, splat_sum(sums[k]), mine_row)
    row1[...] = mine_row

    pl.semaphore_wait(barrier, len(peers))

    for j in range(len(first)):
        remote(row1, got1.at[j], red_send.at[0], red_recv.at[0], first[j]).start()

    keep, give = c * HALF, (1 - c) * HALF

    def swap(k):
        return remote(ls_send.at[k], ls_recv.at[k], swap_sem.at[0, k], swap_sem.at[1, k], core_peer)

    def level_sums(k, _):
        for g in range(2):
            for dst, start in ((ls_send, give), (ls_own, keep)):
                at = pl.ds(pl.multiple_of(start, HALF), HALF)
                dst[k, g] = kv[k, 0, 3 * g, at, :].astype(f32) + kv[k, 1, 3 * g, at, :].astype(f32)
        swap(k).start()
        return 0

    lax.fori_loop(0, KRYLOV, level_sums, 0)

    load_s.wait()
    parts = [sv[3, 0], sv[3, 1], sv[4, 0], sv[4, 1]]
    at_ends = sum(jnp.dot(parts[i], pick_coef[i], preferred_element_type=f32) for i in range(4))
    mixed = None
    for k in range(KRYLOV):
        strips = sum(
            jnp.dot(kv[k, p // FIELDS, p % FIELDS], pick[p], preferred_element_type=f32) for p in range(PAIRS)
        )
        strips = pltpu.roll(strips, 2 * PAIRS * k, 1) if k else strips
        mixed = strips if mixed is None else mixed + strips
    col_mix[...] = mixed * at_ends

    def edge_rows(k, _):
        for p in range(PAIRS):
            lev, f = p // FIELDS, p % FIELDS
            last = sv[1, lev, ROWS - 16 : ROWS, :].astype(f32) * kv[k, lev, f, ROWS - 16 : ROWS, :].astype(f32)
            first = sv[2, lev, 0:16, :].astype(f32) * kv[k, lev, f, 0:16, :].astype(f32)
            row_send[0, pl.ds(k * PAIRS + p, 1), :] = last[15:16]
            row_send[1, pl.ds(k * PAIRS + p, 1), :] = first[0:1]
        return 0

    lax.fori_loop(0, KRYLOV, edge_rows, 0)
    for i in range(2):
        col_t[...] = jnp.transpose(col_mix[i * COLS : (i + 1) * COLS, :])
        for s in range(2):
            col_send[s, :, i * COLS : (i + 1) * COLS] = col_t[pl.ds(s, STRIPS, stride=2), :]

    lane = lax.broadcasted_iota(jnp.int32, (ROWS, COLS), 1)
    row = lax.broadcasted_iota(jnp.int32, (ROWS, COLS), 0)
    for lev in range(LEVELS):
        coef[0, lev] = sv[0, lev].astype(f32)
        coef[1, lev] = jnp.where(row == ROWS - 1, 0.0, sv[1, lev].astype(f32))
        coef[2, lev] = jnp.where(row == 0, 0.0, sv[2, lev].astype(f32))
        coef[3, lev] = jnp.where(lane == COLS - 1, 0.0, sv[3, lev].astype(f32))
        coef[4, lev] = jnp.where(lane == 0, 0.0, sv[4, lev].astype(f32))

    for k in range(KRYLOV):
        swap(k).wait()
        ls_send[k] = ls_own[k] + ls_recv[k]

    def span(j):
        return (j * PART) // HALF, pl.ds((j * PART) % HALF, PART)

    def raw_down(j):
        g, rows = span(j)
        return remote(ls_send.at[:, g, rows], raw_a.at[j], raw_send.at[0, j], raw_a_sem.at[j], below_peer)

    def raw_up(j):
        g, rows = span(j)
        return remote(ls_send.at[:, g, rows], raw_b.at[j], raw_send.at[1, j], raw_b_sem.at[j], above_peer)

    def send_raw(j):
        @pl.when(y >= 2)
        def _():
            raw_down(j).start()

        @pl.when(y == NY - 1)
        def _():
            raw_up(j).start()

    for j in range(EARLIEST):
        send_raw(j)

    pltpu.make_async_copy(got1, got1, red_recv.at[0]).wait()
    stage = row1[...]
    for j in range(len(first)):
        stage = stage + got1[j]
    row2[...] = stage
    for j in range(len(second)):
        remote(row2, got2.at[j], red_send.at[1], red_recv.at[1], second[j]).start()

    edges = [
        remote(src, dst, edge_sem.at[s], edge_sem.at[4 + s], edge_peers[s])
        for s, (src, dst) in enumerate(
            (
                (row_send.at[0], row_got.at[0]),
                (row_send.at[1], row_got.at[1]),
                (col_send.at[0], col_got.at[0]),
                (col_send.at[1], col_got.at[1]),
            )
        )
    ]
    for s in (2, 3, 0, 1):
        edges[s].start()

    for j in range(EARLIEST, EARLY):
        send_raw(j)
    for load in (load_w, load_p, load_t):
        load.wait()
    pltpu.make_async_copy(got1, got1, red_send.at[0]).wait()

    pltpu.make_async_copy(got2, got2, red_recv.at[1]).wait()
    stage = row2[...]
    for j in range(len(second)):
        stage = stage + got2[j]
    coupling = [
        jnp.sum(jnp.where(lane1 == k, stage, 0.0), axis=1, keepdims=True) * (0.5 / COUNT)
        for k in range(KRYLOV)
    ]
    mix, mix_one = [], []
    for j in range(KRYLOV):
        m = proj[0, j] * coupling[0]
        for k in range(1, KRYLOV):
            m = m + proj[k, j] * coupling[k]
        mix_one.append(m)
        mix.append(jnp.broadcast_to(m, (8, COLS)))

    def mixed(parts):
        acc = None
        for m, p in zip(mix, parts):
            term = jnp.concatenate([m] * (p.shape[0] // 8), axis=0) * p
            acc = term if acc is None else acc + term
        return acc

    def down(src, j):
        return remote(src.at[j], buf_a.at[j], y_send.at[0, j], a_sem.at[j], below_peer)

    def up(src, j):
        return remote(src.at[j], buf_b.at[j], y_send.at[1, j], b_sem.at[j], above_peer)

    for j in range(EARLY, CHUNKS):
        g, rows = span(j)
        total[j] = mixed([ls_send[k, g, rows, :] for k in range(KRYLOV)])

        @pl.when(y >= 2)
        def _(j=j):
            down(total, j).start()

        @pl.when(y == NY - 1)
        def _(j=j):
            up(total, j).start()

    def pass_down(j):
        return remote(relay.at[j], buf_b.at[j], y_send.at[0, j], b_sem.at[j], below_peer)

    for j in range(EARLY):
        g, rows = span(j)
        total[j] = mixed([ls_send[k, g, rows, :] for k in range(KRYLOV)])

        @pl.when(y == 2)
        def _(j=j):
            raw_down(j).wait_recv()
            relay[j] = mixed([raw_a[j, k] for k in range(KRYLOV)])
            pass_down(j).start()
            buf_a[j] = relay[j]

        @pl.when(y == 1)
        def _(j=j):
            raw_down(j).wait_recv()
            buf_a[j] = mixed([raw_a[j, k] for k in range(KRYLOV)])
            relay[j] = total[j] + buf_a[j]
            down(relay, j).start()

        @pl.when(y == 0)
        def _(j=j):
            raw_up(j).wait_recv()
            buf_b[j] = mixed([raw_b[j, k] for k in range(KRYLOV)])

    for j in range(CHUNKS):
        g, rows = span(j)
        mine[j] = mixed([ls_own[k, g, rows, :] for k in range(KRYLOV)])

    @pl.when(y == NY - 1)
    def _():
        buf_a[...] = jnp.zeros(buf_a.shape, f32)

    @pl.when(y >= 2)
    def _():
        buf_b[...] = jnp.zeros(buf_b.shape, f32)

    def combine(i, _):
        lev, blk = i // 8, lax.rem(i, 8)
        at = pl.ds(pl.multiple_of(blk * 32, 32), 32)
        for f in range(FIELDS):
            comb[lev * FIELDS + f, at, :] = mixed([kv[k, lev, f, at, :].astype(f32) for k in range(KRYLOV)])
        return 0

    lax.fori_loop(0, LEVELS * 8, combine, 0)

    outer = (lane == 0) | (lane == COLS - 1)

    def interior(p, _):
        lev, f = p // FIELDS, lax.rem(p, FIELDS)
        field = comb[p]
        acc = av[lev, f] + jnp.where(outer, pltpu.roll(col_add[...], COLS - 1 - 2 * p, 1), 0.0)
        acc = acc + coef[0, lev] * field
        acc = acc + pltpu.roll(coef[1, lev] * field, 1, 0)
        acc = acc + pltpu.roll(coef[2, lev] * field, ROWS - 1, 0)
        acc = acc + pltpu.roll(coef[3, lev] * field, 1, 1)
        acc = acc + pltpu.roll(coef[4, lev] * field, COLS - 1, 1)
        out[lev, f] = acc
        out[lev, f, 0:1, :] = acc[0:1] + row_mix[0, pl.ds(p, 1), :]
        out[lev, f, ROWS - 1 : ROWS, :] = acc[ROWS - 1 : ROWS] + row_mix[1, pl.ds(p, 1), :]
        return 0

    def pass_on(j, _):
        @pl.when(y == 1)
        def _():
            down(total, j).wait_recv()
            relay[j] = total[j] + buf_a[j]
            down(relay, j).start()

        @pl.when(y == 0)
        def _():
            up(total, j).wait_recv()
            up(buf_b, j).start()

        return 0

    lax.fori_loop(EARLY, EARLY + 2, pass_on, 0)

    for s in range(4):
        edges[s].wait()

    def mixed_strips(ref, s):
        return sum(mix_one[k] * ref[s, k * PAIRS : (k + 1) * PAIRS, :] for k in range(KRYLOV))

    lane_flip = COLS - 1 - lax.broadcasted_iota(jnp.int32, (16, COLS), 1)
    for s in range(2):
        row_mix[s, 0:PAIRS, :] = mixed_strips(row_got, s)
        strip_mix[s, 0:PAIRS, :] = mixed_strips(col_got, s)
    for s in range(2):
        row_mix[s] = turned(row_mix[s], seam[0, s], lane_flip)[0]
        parts = turned(strip_mix[s], seam[0, 2 + s], lane_flip)
        for i in range(2):
            col_back[i, pl.ds(1 - s, 16, stride=2), :] = parts[i]
    col_add[0:COLS, :] = jnp.transpose(col_back[0])
    col_add[COLS:ROWS, :] = jnp.transpose(col_back[1])

    def pass_and_interior(j, _):
        pass_on(EARLY + 2 + j, 0)
        steps = CHUNKS - EARLY - 2
        lax.fori_loop(j * PAIRS // steps, (j + 1) * PAIRS // steps, interior, 0)
        return 0

    lax.fori_loop(0, CHUNKS - EARLY - 2, pass_and_interior, 0)

    def hand(j):
        return remote(below_send.at[j], below.at[j], below_sem.at[0, j], below_sem.at[1, j], core_peer)

    def integrals(j, start, sums):
        g = (j * PART) // HALF
        at = pl.ds(pl.multiple_of(start + lax.rem(j * PART, HALF), PART), PART)
        upper = sums + comb[FIELDS + 3 * g, at, :]
        lower = upper + comb[3 * g, at, :]
        f = 1 + 3 * g
        out[1, f, at, :] = out[1, f, at, :] + wv[g, 1, at, :] * upper
        out[0, f, at, :] = out[0, f, at, :] + wv[g, 0, at, :] * lower

    def finish_mine(j, _, early=False):
        @pl.when((y == 0) if early else ((y == 2) | (y == 0)))
        def _():
            down(total, j).wait_recv()

        @pl.when(y == 1)
        def _():
            up(total, j).wait_recv()

        higher = buf_a[j] + buf_b[j]
        below_send[j] = jnp.where(c == 1, higher + mine[j], higher)
        hand(j).start()
        integrals(j, keep, jnp.where(c == 1, higher, higher + (total[j] - mine[j])))
        return 0

    def finish_other(j, _):
        hand(j).wait()
        integrals(j, give, below[j])
        return 0

    lax.fori_loop(0, EARLY, lambda j, _: finish_mine(j, 0, True), 0)
    lax.fori_loop(EARLY, CHUNKS, finish_mine, 0)

    def sent(j, _, early=False):
        @pl.when(((y == 1) | (y == 2)) if early else (y >= 1))
        def _():
            down(total, j).wait_send()

        if not early:

            @pl.when((y == NY - 1) | (y == 0))
            def _():
                up(total, j).wait_send()

        return 0

    for j in range(EARLY):

        @pl.when(y >= 2)
        def _(j=j):
            raw_down(j).wait_send()

        @pl.when(y == NY - 1)
        def _(j=j):
            raw_up(j).wait_send()

    lax.fori_loop(0, EARLY, lambda j, _: sent(j, 0, True), 0)
    lax.fori_loop(EARLY, CHUNKS, sent, 0)
    pltpu.make_async_copy(got2, got2, red_send.at[1]).wait()
    lax.fori_loop(0, CHUNKS, finish_other, 0)


def per_device(krylov, adjoint, projected, stencil, column_weight, seam_turns):
    f32 = jnp.float32
    vm = pltpu.VMEM
    dma = pltpu.SemaphoreType.DMA
    part = vm((CHUNKS, PART, COLS), f32)
    raw = vm((EARLY, KRYLOV, PART, COLS), f32)
    sums = vm((KRYLOV, 2, HALF, COLS), f32)
    return pl.pallas_call(
        kernel,
        out_shape=jax.ShapeDtypeStruct(adjoint.shape, f32),
        in_specs=[pl.BlockSpec(memory_space=pltpu.HBM)] * 6,
        out_specs=pl.BlockSpec(memory_space=pltpu.VMEM),
        scratch_shapes=[
            vm(krylov.shape, krylov.dtype), vm(adjoint.shape, f32), vm(stencil.shape, stencil.dtype),
            vm(column_weight.shape, f32),
            pltpu.SMEM(projected.shape, f32), pltpu.SMEM(seam_turns.shape, jnp.int32),
            vm(stencil.shape, f32), vm((PAIRS, ROWS, COLS), f32),
            vm((PAIRS, COLS, COLS), jnp.bfloat16), vm((2 * LEVELS, COLS, COLS), jnp.bfloat16),
            sums, sums, sums, part, part, part, part, part, raw, raw, part, part,
            vm((1, COLS), f32), vm((1, COLS), f32),
            vm((len(FIRST), 1, COLS), f32), vm((len(SECOND), 1, COLS), f32),
            vm((2, STRIPS, COLS), f32), vm((2, STRIPS, COLS), f32), vm((2, 16, COLS), f32), vm((ROWS, COLS), f32),
            vm((COLS, COLS), f32), vm((2, STRIPS, ROWS), f32), vm((2, STRIPS, ROWS), f32), vm((2, 16, ROWS), f32),
            vm((2, COLS, COLS), f32), vm((ROWS, COLS), f32),
            dma((2 * FIELDS + 4,)), dma((2,)), dma((2,)), dma((2, KRYLOV)), dma((2, CHUNKS)), dma((CHUNKS,)),
            dma((CHUNKS,)), dma((2, EARLY)), dma((EARLY,)), dma((EARLY,)), dma((2, CHUNKS)), dma((8,)),
        ],
        name="step",
        compiler_params=pltpu.CompilerParams(
            collective_id=0, has_side_effects=True, vmem_limit_bytes=32 << 20
        ),
    )(
        *[
            pltpu.with_memory_space_constraint(a, pltpu.HBM)
            for a in (krylov, adjoint, stencil, column_weight, projected, seam_turns)
        ]
    )


def solution(mesh):
    placed = (
        P(None, "lev", None, "tile", None),
        P("lev", None, "tile", None),
        P(),
        P(None, "lev", "tile", None),
        P(None, "lev", "tile", None),
        P("tile", None),
    )
    return jax.shard_map(
        per_device,
        mesh=mesh,
        in_specs=placed,
        out_specs=P("lev", None, "tile", None),
        check_vma=False,
    )
```

```python
import jax
import jax.numpy as jnp
from jax import lax
from jax.experimental import pallas as pl
from jax.experimental.pallas import tpu as pltpu
from jax.sharding import PartitionSpec as P

MESH = pl.DeviceIdType.MESH
STRIDE = 4
KRYLOV = 4
FIELDS = 5
LEVELS = 2
ROWS = 256
COLS = 128
HALF = ROWS // 2
NX, NZ, NY, NC = 4, 8, 4, 2
PAIRS = LEVELS * FIELDS
STRIPS = KRYLOV * PAIRS
CHUNKS = 8
PART = 2 * HALF // CHUNKS
EARLY = 4
EARLIEST = 1
COUNT = 16 * FIELDS * 8192 * COLS


def ring(d, n):
    return min(d % n, (-d) % n)


def group(nx, nz, ny, nc):
    offsets = [
        (dx, dz, dy, dc) for dx in range(nx) for dz in range(nz) for dy in range(ny) for dc in range(nc)
    ]
    return sorted(
        offsets[1:], key=lambda o: -(ring(o[0], NX) + ring(o[1], NZ) + ring(o[2], NY) + 0.5 * o[3])
    )


FIRST = group(NX, 1, NY, 1)
SECOND = group(1, NZ, 1, NC)
UNROLL = 16


def splat_sum(x):
    return jnp.sum(jnp.sum(x, axis=0, keepdims=True), axis=1, keepdims=True)


def turned(strip, turn, lane_flip):
    odd = lax.rem(turn, 2) == 1
    cosine = jnp.where(turn == 0, 1.0, jnp.where(turn == 2, -1.0, 0.0)).astype(jnp.float32)
    sine = jnp.where(turn == 1, 1.0, jnp.where(turn == 3, -1.0, 0.0)).astype(jnp.float32)
    halves = [strip[:, i : i + COLS] for i in range(0, strip.shape[1], COLS)]
    back = [jnp.take_along_axis(h, lane_flip, axis=1) for h in halves[::-1]]
    field = lax.rem(lax.broadcasted_iota(jnp.int32, halves[0].shape, 0), FIELDS)
    out = []
    for h, b in zip(halves, back):
        x = jnp.where(odd, b, h)
        after = pltpu.roll(x, x.shape[0] - 1, 0)
        before = pltpu.roll(x, 1, 0)
        out.append(
            jnp.where(
                field == 2,
                cosine * x - sine * after,
                jnp.where(field == 3, sine * before + cosine * x, x),
            )
        )
    return out


def kernel(
    k_hbm, a_hbm, s_hbm, w_hbm, p_hbm, t_hbm,
    out,
    kv, av, sv, wv, proj, seam, coef, comb, pick, pick_coef,
    ls_own, ls_send, ls_recv, total, mine, relay, buf_a, buf_b, raw_a, raw_b, below_send, below,
    row1, row2, got1, got2,
    row_send, row_got, row_mix, col_mix, col_t, col_send, col_got, strip_mix, col_back, col_add,
    load_sem, red_send, red_recv, swap_sem, y_send, a_sem, b_sem, raw_send, raw_a_sem, raw_b_sem, below_sem, edge_sem,
):
    t, l = lax.axis_index("tile"), lax.axis_index("lev")
    x, z, y, c = t // NZ, lax.rem(t, NZ), l // NC, lax.rem(l, NC)
    f32 = jnp.float32

    load_k = [pltpu.make_async_copy(k_hbm.at[:, :, f], kv.at[:, :, f], load_sem.at[f]) for f in range(FIELDS)]
    load_a = [pltpu.make_async_copy(a_hbm.at[:, f], av.at[:, f], load_sem.at[FIELDS + f]) for f in range(FIELDS)]
    load_s = pltpu.make_async_copy(s_hbm, sv, load_sem.at[2 * FIELDS])
    load_w = pltpu.make_async_copy(w_hbm, wv, load_sem.at[2 * FIELDS + 1])
    load_p = pltpu.make_async_copy(p_hbm, proj, load_sem.at[2 * FIELDS + 2])
    load_t = pltpu.make_async_copy(t_hbm, seam, load_sem.at[2 * FIELDS + 3])
    for f in range(FIELDS):
        load_k[f].start()
        load_a[f].start()

    def device(dx, dz, dy, dc):
        return (
            lax.rem(x + dx, NX) * NZ + lax.rem(z + dz, NZ), lax.rem(y + dy, NY) * NC + lax.rem(c + dc, NC)
        )

    def at_tile(d):
        return (lax.rem(t + d + NX * NZ, NX * NZ), l)

    def remote(src, dst, send, recv, where):
        return pltpu.make_async_remote_copy(
            src_ref=src, dst_ref=dst, send_sem=send, recv_sem=recv, device_id=where, device_id_type=MESH
        )

    first, second = [device(*o) for o in FIRST], [device(*o) for o in SECOND]
    core_peer, below_peer, above_peer = device(0, 0, 0, 1), device(0, 0, NY - 1, 0), device(0, 0, 1, 0)
    edge_peers = [at_tile(d) for d in (1, -1, STRIDE, -STRIDE)]
    peers = second + first + edge_peers
    barrier = pltpu.get_barrier_semaphore()
    for peer in peers:
        pl.semaphore_signal(barrier, inc=1, device_id=peer, device_id_type=MESH)
    for load in (load_s, load_w, load_p, load_t):
        load.start()

    li = lax.broadcasted_iota(jnp.int32, (COLS, COLS), 0)
    lj = lax.broadcasted_iota(jnp.int32, (COLS, COLS), 1)

    def store_mask(ref, i, mask):
        ref[i] = jnp.where(mask, 1.0, 0.0).astype(jnp.bfloat16)

    for p in range(PAIRS):
        store_mask(pick, p, ((li == COLS - 1) & (lj == 2 * p)) | ((li == 0) & (lj == 2 * p + 1)))
    pair = lax.rem(lj, 2 * PAIRS)
    for lev in range(LEVELS):
        here = (pair >= 2 * FIELDS * lev) & (pair < 2 * FIELDS * (lev + 1)) & (lj < 2 * STRIPS)
        store_mask(pick_coef, lev, here & (li == COLS - 1) & (lax.rem(lj, 2) == 0))
        store_mask(pick_coef, LEVELS + lev, here & (li == 0) & (lax.rem(lj, 2) == 1))

    sums = (jnp.zeros((16, COLS), f32),) * KRYLOV
    for f in range(FIELDS):
        load_k[f].wait()
        load_a[f].wait()

        def dots(i, sums, f=f):
            lev, blk = i // 16, lax.rem(i, 16)
            at = pl.ds(pl.multiple_of(blk * 16, 16), 16)
            a = av[lev, f, at, :]
            return tuple(sums[k] + kv[k, lev, f, at, :].astype(f32) * a for k in range(KRYLOV))

        sums = lax.fori_loop(0, LEVELS * 16, dots, sums, unroll=UNROLL)

    lane1 = lax.broadcasted_iota(jnp.int32, (1, COLS), 1)
    mine_row = jnp.zeros((1, COLS), f32)
    for k in range(KRYLOV):
        mine_row = jnp.where(lane1 == k, splat_sum(sums[k]), mine_row)
    row1[...] = mine_row

    pl.semaphore_wait(barrier, len(peers))

    for j in range(len(first)):
        remote(row1, got1.at[j], red_send.at[0], red_recv.at[0], first[j]).start()

    keep, give = c * HALF, (1 - c) * HALF

    def swap(k):
        return remote(ls_send.at[k], ls_recv.at[k], swap_sem.at[0, k], swap_sem.at[1, k], core_peer)

    def level_sums(k, _):
        for g in range(2):
            for dst, start in ((ls_send, give), (ls_own, keep)):
                at = pl.ds(pl.multiple_of(start, HALF), HALF)
                dst[k, g] = kv[k, 0, 3 * g, at, :].astype(f32) + kv[k, 1, 3 * g, at, :].astype(f32)
        swap(k).start()
        return 0

    lax.fori_loop(0, KRYLOV, level_sums, 0)

    load_s.wait()
    parts = [sv[3, 0], sv[3, 1], sv[4, 0], sv[4, 1]]
    at_ends = sum(jnp.dot(parts[i], pick_coef[i], preferred_element_type=f32) for i in range(4))
    mixed = None
    for k in range(KRYLOV):
        strips = sum(
            jnp.dot(kv[k, p // FIELDS, p % FIELDS], pick[p], preferred_element_type=f32) for p in range(PAIRS)
        )
        strips = pltpu.roll(strips, 2 * PAIRS * k, 1) if k else strips
        mixed = strips if mixed is None else mixed + strips
    col_mix[...] = mixed * at_ends

    def edge_rows(k, _):
        for p in range(PAIRS):
            lev, f = p // FIELDS, p % FIELDS
            last = sv[1, lev, ROWS - 16 : ROWS, :].astype(f32) * kv[k, lev, f, ROWS - 16 : ROWS, :].astype(f32)
            first = sv[2, lev, 0:16, :].astype(f32) * kv[k, lev, f, 0:16, :].astype(f32)
            row_send[0, pl.ds(k * PAIRS + p, 1), :] = last[15:16]
            row_send[1, pl.ds(k * PAIRS + p, 1), :] = first[0:1]
        return 0

    lax.fori_loop(0, KRYLOV, edge_rows, 0)
    for i in range(2):
        col_t[...] = jnp.transpose(col_mix[i * COLS : (i + 1) * COLS, :])
        for s in range(2):
            col_send[s, :, i * COLS : (i + 1) * COLS] = col_t[pl.ds(s, STRIPS, stride=2), :]

    lane = lax.broadcasted_iota(jnp.int32, (ROWS, COLS), 1)
    row = lax.broadcasted_iota(jnp.int32, (ROWS, COLS), 0)
    for lev in range(LEVELS):
        coef[0, lev] = sv[0, lev].astype(f32)
        coef[1, lev] = jnp.where(row == ROWS - 1, 0.0, sv[1, lev].astype(f32))
        coef[2, lev] = jnp.where(row == 0, 0.0, sv[2, lev].astype(f32))
        coef[3, lev] = jnp.where(lane == COLS - 1, 0.0, sv[3, lev].astype(f32))
        coef[4, lev] = jnp.where(lane == 0, 0.0, sv[4, lev].astype(f32))

    for k in range(KRYLOV):
        swap(k).wait()
        ls_send[k] = ls_own[k] + ls_recv[k]

    def span(j):
        return (j * PART) // HALF, pl.ds((j * PART) % HALF, PART)

    def raw_down(j):
        g, rows = span(j)
        return remote(ls_send.at[:, g, rows], raw_a.at[j], raw_send.at[0, j], raw_a_sem.at[j], below_peer)

    def raw_up(j):
        g, rows = span(j)
        return remote(ls_send.at[:, g, rows], raw_b.at[j], raw_send.at[1, j], raw_b_sem.at[j], above_peer)

    def send_raw(j):
        @pl.when(y >= 2)
        def _():
            raw_down(j).start()

        @pl.when(y == NY - 1)
        def _():
            raw_up(j).start()

    for j in range(EARLIEST):
        send_raw(j)

    pltpu.make_async_copy(got1, got1, red_recv.at[0]).wait()
    stage = row1[...]
    for j in range(len(first)):
        stage = stage + got1[j]
    row2[...] = stage
    for j in range(len(second)):
        remote(row2, got2.at[j], red_send.at[1], red_recv.at[1], second[j]).start()

    edges = [
        remote(src, dst, edge_sem.at[s], edge_sem.at[4 + s], edge_peers[s])
        for s, (src, dst) in enumerate(
            (
                (row_send.at[0], row_got.at[0]),
                (row_send.at[1], row_got.at[1]),
                (col_send.at[0], col_got.at[0]),
                (col_send.at[1], col_got.at[1]),
            )
        )
    ]
    for s in (2, 3, 0, 1):
        edges[s].start()

    for j in range(EARLIEST, EARLY):
        send_raw(j)
    for load in (load_w, load_p, load_t):
        load.wait()
    pltpu.make_async_copy(got1, got1, red_send.at[0]).wait()

    pltpu.make_async_copy(got2, got2, red_recv.at[1]).wait()
    stage = row2[...]
    for j in range(len(second)):
        stage = stage + got2[j]
    coupling = [
        jnp.sum(jnp.where(lane1 == k, stage, 0.0), axis=1, keepdims=True) * (0.5 / COUNT)
        for k in range(KRYLOV)
    ]
    mix, mix_one = [], []
    for j in range(KRYLOV):
        m = proj[0, j] * coupling[0]
        for k in range(1, KRYLOV):
            m = m + proj[k, j] * coupling[k]
        mix_one.append(m)
        mix.append(jnp.broadcast_to(m, (8, COLS)))

    def mixed(parts):
        acc = None
        for m, p in zip(mix, parts):
            term = jnp.concatenate([m] * (p.shape[0] // 8), axis=0) * p
            acc = term if acc is None else acc + term
        return acc

    def down(src, j):
        return remote(src.at[j], buf_a.at[j], y_send.at[0, j], a_sem.at[j], below_peer)

    def up(src, j):
        return remote(src.at[j], buf_b.at[j], y_send.at[1, j], b_sem.at[j], above_peer)

    for j in range(EARLY, CHUNKS):
        g, rows = span(j)
        total[j] = mixed([ls_send[k, g, rows, :] for k in range(KRYLOV)])

        @pl.when(y >= 2)
        def _(j=j):
            down(total, j).start()

        @pl.when(y == NY - 1)
        def _(j=j):
            up(total, j).start()

    def pass_down(j):
        return remote(relay.at[j], buf_b.at[j], y_send.at[0, j], b_sem.at[j], below_peer)

    for j in range(EARLY):
        g, rows = span(j)
        total[j] = mixed([ls_send[k, g, rows, :] for k in range(KRYLOV)])

        @pl.when(y == 2)
        def _(j=j):
            raw_down(j).wait_recv()
            relay[j] = mixed([raw_a[j, k] for k in range(KRYLOV)])
            pass_down(j).start()
            buf_a[j] = relay[j]

        @pl.when(y == 1)
        def _(j=j):
            raw_down(j).wait_recv()
            buf_a[j] = mixed([raw_a[j, k] for k in range(KRYLOV)])
            relay[j] = total[j] + buf_a[j]
            down(relay, j).start()

        @pl.when(y == 0)
        def _(j=j):
            raw_up(j).wait_recv()
            buf_b[j] = mixed([raw_b[j, k] for k in range(KRYLOV)])

    for j in range(CHUNKS):
        g, rows = span(j)
        mine[j] = mixed([ls_own[k, g, rows, :] for k in range(KRYLOV)])

    @pl.when(y == NY - 1)
    def _():
        buf_a[...] = jnp.zeros(buf_a.shape, f32)

    @pl.when(y >= 2)
    def _():
        buf_b[...] = jnp.zeros(buf_b.shape, f32)

    def combine(i, _):
        lev, blk = i // 8, lax.rem(i, 8)
        at = pl.ds(pl.multiple_of(blk * 32, 32), 32)
        for f in range(FIELDS):
            comb[lev * FIELDS + f, at, :] = mixed([kv[k, lev, f, at, :].astype(f32) for k in range(KRYLOV)])
        return 0

    lax.fori_loop(0, LEVELS * 8, combine, 0)

    outer = (lane == 0) | (lane == COLS - 1)

    def interior(p, _):
        lev, f = p // FIELDS, lax.rem(p, FIELDS)
        field = comb[p]
        acc = av[lev, f] + jnp.where(outer, pltpu.roll(col_add[...], COLS - 1 - 2 * p, 1), 0.0)
        acc = acc + coef[0, lev] * field
        acc = acc + pltpu.roll(coef[1, lev] * field, 1, 0)
        acc = acc + pltpu.roll(coef[2, lev] * field, ROWS - 1, 0)
        acc = acc + pltpu.roll(coef[3, lev] * field, 1, 1)
        acc = acc + pltpu.roll(coef[4, lev] * field, COLS - 1, 1)
        out[lev, f] = acc
        out[lev, f, 0:1, :] = acc[0:1] + row_mix[0, pl.ds(p, 1), :]
        out[lev, f, ROWS - 1 : ROWS, :] = acc[ROWS - 1 : ROWS] + row_mix[1, pl.ds(p, 1), :]
        return 0

    def pass_on(j, _):
        @pl.when(y == 1)
        def _():
            down(total, j).wait_recv()
            relay[j] = total[j] + buf_a[j]
            down(relay, j).start()

        @pl.when(y == 0)
        def _():
            up(total, j).wait_recv()
            up(buf_b, j).start()

        return 0

    lax.fori_loop(EARLY, CHUNKS, pass_on, 0)

    for s in range(4):
        edges[s].wait()

    def mixed_strips(ref, s):
        return sum(mix_one[k] * ref[s, k * PAIRS : (k + 1) * PAIRS, :] for k in range(KRYLOV))

    lane_flip = COLS - 1 - lax.broadcasted_iota(jnp.int32, (16, COLS), 1)
    for s in range(2):
        row_mix[s, 0:PAIRS, :] = mixed_strips(row_got, s)
        strip_mix[s, 0:PAIRS, :] = mixed_strips(col_got, s)
    for s in range(2):
        row_mix[s] = turned(row_mix[s], seam[0, s], lane_flip)[0]
        parts = turned(strip_mix[s], seam[0, 2 + s], lane_flip)
        for i in range(2):
            col_back[i, pl.ds(1 - s, 16, stride=2), :] = parts[i]
    col_add[0:COLS, :] = jnp.transpose(col_back[0])
    col_add[COLS:ROWS, :] = jnp.transpose(col_back[1])

    lax.fori_loop(0, PAIRS, interior, 0)

    def hand(j):
        return remote(below_send.at[j], below.at[j], below_sem.at[0, j], below_sem.at[1, j], core_peer)

    def integrals(j, start, sums):
        g = (j * PART) // HALF
        at = pl.ds(pl.multiple_of(start + lax.rem(j * PART, HALF), PART), PART)
        upper = sums + comb[FIELDS + 3 * g, at, :]
        lower = upper + comb[3 * g, at, :]
        f = 1 + 3 * g
        out[1, f, at, :] = out[1, f, at, :] + wv[g, 1, at, :] * upper
        out[0, f, at, :] = out[0, f, at, :] + wv[g, 0, at, :] * lower

    def finish_mine(j, _, early=False):
        @pl.when((y == 0) if early else ((y == 2) | (y == 0)))
        def _():
            down(total, j).wait_recv()

        @pl.when(y == 1)
        def _():
            up(total, j).wait_recv()

        higher = buf_a[j] + buf_b[j]
        below_send[j] = jnp.where(c == 1, higher + mine[j], higher)
        hand(j).start()
        integrals(j, keep, jnp.where(c == 1, higher, higher + (total[j] - mine[j])))
        return 0

    def finish_other(j, _):
        hand(j).wait()
        integrals(j, give, below[j])
        return 0

    lax.fori_loop(0, EARLY, lambda j, _: finish_mine(j, 0, True), 0)
    lax.fori_loop(EARLY, CHUNKS, finish_mine, 0)

    def sent(j, _, early=False):
        @pl.when(((y == 1) | (y == 2)) if early else (y >= 1))
        def _():
            down(total, j).wait_send()

        if not early:

            @pl.when((y == NY - 1) | (y == 0))
            def _():
                up(total, j).wait_send()

        return 0

    for j in range(EARLY):

        @pl.when(y >= 2)
        def _(j=j):
            raw_down(j).wait_send()

        @pl.when(y == NY - 1)
        def _(j=j):
            raw_up(j).wait_send()

    lax.fori_loop(0, EARLY, lambda j, _: sent(j, 0, True), 0)
    lax.fori_loop(EARLY, CHUNKS, sent, 0)
    pltpu.make_async_copy(got2, got2, red_send.at[1]).wait()
    lax.fori_loop(0, CHUNKS, finish_other, 0)


def per_device(krylov, adjoint, projected, stencil, column_weight, seam_turns):
    f32 = jnp.float32
    vm = pltpu.VMEM
    dma = pltpu.SemaphoreType.DMA
    part = vm((CHUNKS, PART, COLS), f32)
    raw = vm((EARLY, KRYLOV, PART, COLS), f32)
    sums = vm((KRYLOV, 2, HALF, COLS), f32)
    return pl.pallas_call(
        kernel,
        out_shape=jax.ShapeDtypeStruct(adjoint.shape, f32),
        in_specs=[pl.BlockSpec(memory_space=pltpu.HBM)] * 6,
        out_specs=pl.BlockSpec(memory_space=pltpu.VMEM),
        scratch_shapes=[
            vm(krylov.shape, krylov.dtype), vm(adjoint.shape, f32), vm(stencil.shape, stencil.dtype),
            vm(column_weight.shape, f32),
            pltpu.SMEM(projected.shape, f32), pltpu.SMEM(seam_turns.shape, jnp.int32),
            vm(stencil.shape, f32), vm((PAIRS, ROWS, COLS), f32),
            vm((PAIRS, COLS, COLS), jnp.bfloat16), vm((2 * LEVELS, COLS, COLS), jnp.bfloat16),
            sums, sums, sums, part, part, part, part, part, raw, raw, part, part,
            vm((1, COLS), f32), vm((1, COLS), f32),
            vm((len(FIRST), 1, COLS), f32), vm((len(SECOND), 1, COLS), f32),
            vm((2, STRIPS, COLS), f32), vm((2, STRIPS, COLS), f32), vm((2, 16, COLS), f32), vm((ROWS, COLS), f32),
            vm((COLS, COLS), f32), vm((2, STRIPS, ROWS), f32), vm((2, STRIPS, ROWS), f32), vm((2, 16, ROWS), f32),
            vm((2, COLS, COLS), f32), vm((ROWS, COLS), f32),
            dma((2 * FIELDS + 4,)), dma((2,)), dma((2,)), dma((2, KRYLOV)), dma((2, CHUNKS)), dma((CHUNKS,)),
            dma((CHUNKS,)), dma((2, EARLY)), dma((EARLY,)), dma((EARLY,)), dma((2, CHUNKS)), dma((8,)),
        ],
        name="step",
        compiler_params=pltpu.CompilerParams(
            collective_id=0, has_side_effects=True, vmem_limit_bytes=32 << 20
        ),
    )(
        *[
            pltpu.with_memory_space_constraint(a, pltpu.HBM)
            for a in (krylov, adjoint, stencil, column_weight, projected, seam_turns)
        ]
    )


def solution(mesh):
    placed = (
        P(None, "lev", None, "tile", None),
        P("lev", None, "tile", None),
        P(),
        P(None, "lev", "tile", None),
        P(None, "lev", "tile", None),
        P("tile", None),
    )
    return jax.shard_map(
        per_device,
        mesh=mesh,
        in_specs=placed,
        out_specs=P("lev", None, "tile", None),
        check_vma=False,
    )
```

```python
import jax
import jax.numpy as jnp
from jax import lax
from jax.experimental import pallas as pl
from jax.experimental.pallas import tpu as pltpu
from jax.sharding import PartitionSpec as P

MESH = pl.DeviceIdType.MESH
STRIDE = 4
KRYLOV = 4
FIELDS = 5
LEVELS = 2
ROWS = 256
COLS = 128
HALF = ROWS // 2
NX, NZ, NY, NC = 4, 8, 4, 2
PAIRS = LEVELS * FIELDS
STRIPS = KRYLOV * PAIRS
CHUNKS = 8
PART = 2 * HALF // CHUNKS
EARLY = 4
EARLIEST = 1
COUNT = 16 * FIELDS * 8192 * COLS


def ring(d, n):
    return min(d % n, (-d) % n)


def group(nx, nz, ny, nc):
    offsets = [
        (dx, dz, dy, dc) for dx in range(nx) for dz in range(nz) for dy in range(ny) for dc in range(nc)
    ]
    return sorted(
        offsets[1:], key=lambda o: -(ring(o[0], NX) + ring(o[1], NZ) + ring(o[2], NY) + 0.5 * o[3])
    )


FIRST = group(NX, 1, NY, 1)
SECOND = group(1, NZ, 1, NC)
UNROLL = 16


def splat_sum(x):
    return jnp.sum(jnp.sum(x, axis=0, keepdims=True), axis=1, keepdims=True)


def turned(strip, turn, lane_flip):
    odd = lax.rem(turn, 2) == 1
    cosine = jnp.where(turn == 0, 1.0, jnp.where(turn == 2, -1.0, 0.0)).astype(jnp.float32)
    sine = jnp.where(turn == 1, 1.0, jnp.where(turn == 3, -1.0, 0.0)).astype(jnp.float32)
    halves = [strip[:, i : i + COLS] for i in range(0, strip.shape[1], COLS)]
    back = [jnp.take_along_axis(h, lane_flip, axis=1) for h in halves[::-1]]
    field = lax.rem(lax.broadcasted_iota(jnp.int32, halves[0].shape, 0), FIELDS)
    out = []
    for h, b in zip(halves, back):
        x = jnp.where(odd, b, h)
        after = pltpu.roll(x, x.shape[0] - 1, 0)
        before = pltpu.roll(x, 1, 0)
        out.append(
            jnp.where(
                field == 2,
                cosine * x - sine * after,
                jnp.where(field == 3, sine * before + cosine * x, x),
            )
        )
    return out


def kernel(
    k_hbm, a_hbm, s_hbm, w_hbm, p_hbm, t_hbm,
    out,
    kv, av, sv, wv, proj, seam, coef, comb, pick, pick_coef,
    ls_own, ls_send, ls_recv, total, mine, relay, buf_a, buf_b, raw_a, raw_b, below_send, below,
    row1, row2, got1, got2,
    row_send, row_got, row_mix, col_mix, col_t, col_send, col_got, strip_mix, col_back, col_add,
    load_sem, red_send, red_recv, swap_sem, y_send, a_sem, b_sem, raw_send, raw_a_sem, raw_b_sem, below_sem, edge_sem,
):
    t, l = lax.axis_index("tile"), lax.axis_index("lev")
    x, z, y, c = t // NZ, lax.rem(t, NZ), l // NC, lax.rem(l, NC)
    f32 = jnp.float32

    load_k = [pltpu.make_async_copy(k_hbm.at[:, :, f], kv.at[:, :, f], load_sem.at[f]) for f in range(FIELDS)]
    load_a = [pltpu.make_async_copy(a_hbm.at[:, f], av.at[:, f], load_sem.at[FIELDS + f]) for f in range(FIELDS)]
    load_s = pltpu.make_async_copy(s_hbm, sv, load_sem.at[2 * FIELDS])
    load_w = pltpu.make_async_copy(w_hbm, wv, load_sem.at[2 * FIELDS + 1])
    load_p = pltpu.make_async_copy(p_hbm, proj, load_sem.at[2 * FIELDS + 2])
    load_t = pltpu.make_async_copy(t_hbm, seam, load_sem.at[2 * FIELDS + 3])
    for f in range(FIELDS):
        load_k[f].start()
        load_a[f].start()

    def device(dx, dz, dy, dc):
        return (
            lax.rem(x + dx, NX) * NZ + lax.rem(z + dz, NZ), lax.rem(y + dy, NY) * NC + lax.rem(c + dc, NC)
        )

    def at_tile(d):
        return (lax.rem(t + d + NX * NZ, NX * NZ), l)

    def remote(src, dst, send, recv, where):
        return pltpu.make_async_remote_copy(
            src_ref=src, dst_ref=dst, send_sem=send, recv_sem=recv, device_id=where, device_id_type=MESH
        )

    first, second = [device(*o) for o in FIRST], [device(*o) for o in SECOND]
    core_peer, below_peer, above_peer = device(0, 0, 0, 1), device(0, 0, NY - 1, 0), device(0, 0, 1, 0)
    edge_peers = [at_tile(d) for d in (1, -1, STRIDE, -STRIDE)]
    peers = second + first
    barrier = pltpu.get_barrier_semaphore()
    for peer in peers:
        pl.semaphore_signal(barrier, inc=1, device_id=peer, device_id_type=MESH)
    for load in (load_s, load_w, load_p, load_t):
        load.start()

    li = lax.broadcasted_iota(jnp.int32, (COLS, COLS), 0)
    lj = lax.broadcasted_iota(jnp.int32, (COLS, COLS), 1)

    def store_mask(ref, i, mask):
        ref[i] = jnp.where(mask, 1.0, 0.0).astype(jnp.bfloat16)

    for p in range(PAIRS):
        store_mask(pick, p, ((li == COLS - 1) & (lj == 2 * p)) | ((li == 0) & (lj == 2 * p + 1)))
    pair = lax.rem(lj, 2 * PAIRS)
    for lev in range(LEVELS):
        here = (pair >= 2 * FIELDS * lev) & (pair < 2 * FIELDS * (lev + 1)) & (lj < 2 * STRIPS)
        store_mask(pick_coef, lev, here & (li == COLS - 1) & (lax.rem(lj, 2) == 0))
        store_mask(pick_coef, LEVELS + lev, here & (li == 0) & (lax.rem(lj, 2) == 1))

    sums = (jnp.zeros((16, COLS), f32),) * KRYLOV
    for f in range(FIELDS):
        load_k[f].wait()
        load_a[f].wait()

        def dots(i, sums, f=f):
            lev, blk = i // 16, lax.rem(i, 16)
            at = pl.ds(pl.multiple_of(blk * 16, 16), 16)
            a = av[lev, f, at, :]
            return tuple(sums[k] + kv[k, lev, f, at, :].astype(f32) * a for k in range(KRYLOV))

        sums = lax.fori_loop(0, LEVELS * 16, dots, sums, unroll=UNROLL)

    lane1 = lax.broadcasted_iota(jnp.int32, (1, COLS), 1)
    mine_row = jnp.zeros((1, COLS), f32)
    for k in range(KRYLOV):
        mine_row = jnp.where(lane1 == k, splat_sum(sums[k]), mine_row)
    row1[...] = mine_row

    pl.semaphore_wait(barrier, len(peers))

    for j in range(len(first)):
        remote(row1, got1.at[j], red_send.at[0], red_recv.at[0], first[j]).start()

    keep, give = c * HALF, (1 - c) * HALF

    def swap(k):
        return remote(ls_send.at[k], ls_recv.at[k], swap_sem.at[0, k], swap_sem.at[1, k], core_peer)

    def level_sums(k, _):
        for g in range(2):
            for dst, start in ((ls_send, give), (ls_own, keep)):
                at = pl.ds(pl.multiple_of(start, HALF), HALF)
                dst[k, g] = kv[k, 0, 3 * g, at, :].astype(f32) + kv[k, 1, 3 * g, at, :].astype(f32)
        swap(k).start()
        return 0

    lax.fori_loop(0, KRYLOV, level_sums, 0)

    load_s.wait()
    parts = [sv[3, 0], sv[3, 1], sv[4, 0], sv[4, 1]]
    at_ends = sum(jnp.dot(parts[i], pick_coef[i], preferred_element_type=f32) for i in range(4))
    mixed = None
    for k in range(KRYLOV):
        strips = sum(
            jnp.dot(kv[k, p // FIELDS, p % FIELDS], pick[p], preferred_element_type=f32) for p in range(PAIRS)
        )
        strips = pltpu.roll(strips, 2 * PAIRS * k, 1) if k else strips
        mixed = strips if mixed is None else mixed + strips
    col_mix[...] = mixed * at_ends

    def edge_rows(k, _):
        for p in range(PAIRS):
            lev, f = p // FIELDS, p % FIELDS
            last = sv[1, lev, ROWS - 16 : ROWS, :].astype(f32) * kv[k, lev, f, ROWS - 16 : ROWS, :].astype(f32)
            first = sv[2, lev, 0:16, :].astype(f32) * kv[k, lev, f, 0:16, :].astype(f32)
            row_send[0, pl.ds(k * PAIRS + p, 1), :] = last[15:16]
            row_send[1, pl.ds(k * PAIRS + p, 1), :] = first[0:1]
        return 0

    lax.fori_loop(0, KRYLOV, edge_rows, 0)
    for i in range(2):
        col_t[...] = jnp.transpose(col_mix[i * COLS : (i + 1) * COLS, :])
        for s in range(2):
            col_send[s, :, i * COLS : (i + 1) * COLS] = col_t[pl.ds(s, STRIPS, stride=2), :]

    lane = lax.broadcasted_iota(jnp.int32, (ROWS, COLS), 1)
    row = lax.broadcasted_iota(jnp.int32, (ROWS, COLS), 0)
    for lev in range(LEVELS):
        coef[0, lev] = sv[0, lev].astype(f32)
        coef[1, lev] = jnp.where(row == ROWS - 1, 0.0, sv[1, lev].astype(f32))
        coef[2, lev] = jnp.where(row == 0, 0.0, sv[2, lev].astype(f32))
        coef[3, lev] = jnp.where(lane == COLS - 1, 0.0, sv[3, lev].astype(f32))
        coef[4, lev] = jnp.where(lane == 0, 0.0, sv[4, lev].astype(f32))

    for k in range(KRYLOV):
        swap(k).wait()
        ls_send[k] = ls_own[k] + ls_recv[k]

    def span(j):
        return (j * PART) // HALF, pl.ds((j * PART) % HALF, PART)

    def raw_down(j):
        g, rows = span(j)
        return remote(ls_send.at[:, g, rows], raw_a.at[j], raw_send.at[0, j], raw_a_sem.at[j], below_peer)

    def raw_up(j):
        g, rows = span(j)
        return remote(ls_send.at[:, g, rows], raw_b.at[j], raw_send.at[1, j], raw_b_sem.at[j], above_peer)

    def send_raw(j):
        @pl.when(y >= 2)
        def _():
            raw_down(j).start()

        @pl.when(y == NY - 1)
        def _():
            raw_up(j).start()

    for j in range(EARLIEST):
        send_raw(j)

    pltpu.make_async_copy(got1, got1, red_recv.at[0]).wait()
    stage = row1[...]
    for j in range(len(first)):
        stage = stage + got1[j]
    row2[...] = stage
    for j in range(len(second)):
        remote(row2, got2.at[j], red_send.at[1], red_recv.at[1], second[j]).start()

    edges = [
        remote(src, dst, edge_sem.at[s], edge_sem.at[4 + s], edge_peers[s])
        for s, (src, dst) in enumerate(
            (
                (row_send.at[0], row_got.at[0]),
                (row_send.at[1], row_got.at[1]),
                (col_send.at[0], col_got.at[0]),
                (col_send.at[1], col_got.at[1]),
            )
        )
    ]
    for s in (2, 3, 0, 1):
        edges[s].start()

    for j in range(EARLIEST, EARLY):
        send_raw(j)
    for load in (load_w, load_p, load_t):
        load.wait()
    pltpu.make_async_copy(got1, got1, red_send.at[0]).wait()

    pltpu.make_async_copy(got2, got2, red_recv.at[1]).wait()
    stage = row2[...]
    for j in range(len(second)):
        stage = stage + got2[j]
    coupling = [
        jnp.sum(jnp.where(lane1 == k, stage, 0.0), axis=1, keepdims=True) * (0.5 / COUNT)
        for k in range(KRYLOV)
    ]
    mix, mix_one = [], []
    for j in range(KRYLOV):
        m = proj[0, j] * coupling[0]
        for k in range(1, KRYLOV):
            m = m + proj[k, j] * coupling[k]
        mix_one.append(m)
        mix.append(jnp.broadcast_to(m, (8, COLS)))

    def mixed(parts):
        acc = None
        for m, p in zip(mix, parts):
            term = jnp.concatenate([m] * (p.shape[0] // 8), axis=0) * p
            acc = term if acc is None else acc + term
        return acc

    def down(src, j):
        return remote(src.at[j], buf_a.at[j], y_send.at[0, j], a_sem.at[j], below_peer)

    def up(src, j):
        return remote(src.at[j], buf_b.at[j], y_send.at[1, j], b_sem.at[j], above_peer)

    for j in range(EARLY, CHUNKS):
        g, rows = span(j)
        total[j] = mixed([ls_send[k, g, rows, :] for k in range(KRYLOV)])

        @pl.when(y >= 2)
        def _(j=j):
            down(total, j).start()

        @pl.when(y == NY - 1)
        def _(j=j):
            up(total, j).start()

    def pass_down(j):
        return remote(relay.at[j], buf_b.at[j], y_send.at[0, j], b_sem.at[j], below_peer)

    for j in range(EARLY):
        g, rows = span(j)
        total[j] = mixed([ls_send[k, g, rows, :] for k in range(KRYLOV)])

        @pl.when(y == 2)
        def _(j=j):
            raw_down(j).wait_recv()
            relay[j] = mixed([raw_a[j, k] for k in range(KRYLOV)])
            pass_down(j).start()
            buf_a[j] = relay[j]

        @pl.when(y == 1)
        def _(j=j):
            raw_down(j).wait_recv()
            buf_a[j] = mixed([raw_a[j, k] for k in range(KRYLOV)])
            relay[j] = total[j] + buf_a[j]
            down(relay, j).start()

        @pl.when(y == 0)
        def _(j=j):
            raw_up(j).wait_recv()
            buf_b[j] = mixed([raw_b[j, k] for k in range(KRYLOV)])

    for j in range(CHUNKS):
        g, rows = span(j)
        mine[j] = mixed([ls_own[k, g, rows, :] for k in range(KRYLOV)])

    @pl.when(y == NY - 1)
    def _():
        buf_a[...] = jnp.zeros(buf_a.shape, f32)

    @pl.when(y >= 2)
    def _():
        buf_b[...] = jnp.zeros(buf_b.shape, f32)

    def combine(i, _):
        lev, blk = i // 8, lax.rem(i, 8)
        at = pl.ds(pl.multiple_of(blk * 32, 32), 32)
        for f in range(FIELDS):
            comb[lev * FIELDS + f, at, :] = mixed([kv[k, lev, f, at, :].astype(f32) for k in range(KRYLOV)])
        return 0

    lax.fori_loop(0, LEVELS * 8, combine, 0)

    outer = (lane == 0) | (lane == COLS - 1)

    def interior(p, _):
        lev, f = p // FIELDS, lax.rem(p, FIELDS)
        field = comb[p]
        acc = av[lev, f] + jnp.where(outer, pltpu.roll(col_add[...], COLS - 1 - 2 * p, 1), 0.0)
        acc = acc + coef[0, lev] * field
        acc = acc + pltpu.roll(coef[1, lev] * field, 1, 0)
        acc = acc + pltpu.roll(coef[2, lev] * field, ROWS - 1, 0)
        acc = acc + pltpu.roll(coef[3, lev] * field, 1, 1)
        acc = acc + pltpu.roll(coef[4, lev] * field, COLS - 1, 1)
        out[lev, f] = acc
        out[lev, f, 0:1, :] = acc[0:1] + row_mix[0, pl.ds(p, 1), :]
        out[lev, f, ROWS - 1 : ROWS, :] = acc[ROWS - 1 : ROWS] + row_mix[1, pl.ds(p, 1), :]
        return 0

    def pass_on(j, _):
        @pl.when(y == 1)
        def _():
            down(total, j).wait_recv()
            relay[j] = total[j] + buf_a[j]
            down(relay, j).start()

        @pl.when(y == 0)
        def _():
            up(total, j).wait_recv()
            up(buf_b, j).start()

        return 0

    lax.fori_loop(EARLY, CHUNKS, pass_on, 0)

    for s in range(4):
        edges[s].wait()

    def mixed_strips(ref, s):
        return sum(mix_one[k] * ref[s, k * PAIRS : (k + 1) * PAIRS, :] for k in range(KRYLOV))

    lane_flip = COLS - 1 - lax.broadcasted_iota(jnp.int32, (16, COLS), 1)
    for s in range(2):
        row_mix[s, 0:PAIRS, :] = mixed_strips(row_got, s)
        strip_mix[s, 0:PAIRS, :] = mixed_strips(col_got, s)
    for s in range(2):
        row_mix[s] = turned(row_mix[s], seam[0, s], lane_flip)[0]
        parts = turned(strip_mix[s], seam[0, 2 + s], lane_flip)
        for i in range(2):
            col_back[i, pl.ds(1 - s, 16, stride=2), :] = parts[i]
    col_add[0:COLS, :] = jnp.transpose(col_back[0])
    col_add[COLS:ROWS, :] = jnp.transpose(col_back[1])

    lax.fori_loop(0, PAIRS, interior, 0)

    def hand(j):
        return remote(below_send.at[j], below.at[j], below_sem.at[0, j], below_sem.at[1, j], core_peer)

    def integrals(j, start, sums):
        g = (j * PART) // HALF
        at = pl.ds(pl.multiple_of(start + lax.rem(j * PART, HALF), PART), PART)
        upper = sums + comb[FIELDS + 3 * g, at, :]
        lower = upper + comb[3 * g, at, :]
        f = 1 + 3 * g
        out[1, f, at, :] = out[1, f, at, :] + wv[g, 1, at, :] * upper
        out[0, f, at, :] = out[0, f, at, :] + wv[g, 0, at, :] * lower

    def finish_mine(j, _, early=False):
        @pl.when((y == 0) if early else ((y == 2) | (y == 0)))
        def _():
            down(total, j).wait_recv()

        @pl.when(y == 1)
        def _():
            up(total, j).wait_recv()

        higher = buf_a[j] + buf_b[j]
        below_send[j] = jnp.where(c == 1, higher + mine[j], higher)
        hand(j).start()
        integrals(j, keep, jnp.where(c == 1, higher, higher + (total[j] - mine[j])))
        return 0

    def finish_other(j, _):
        hand(j).wait()
        integrals(j, give, below[j])
        return 0

    lax.fori_loop(0, EARLY, lambda j, _: finish_mine(j, 0, True), 0)
    lax.fori_loop(EARLY, CHUNKS, finish_mine, 0)

    def sent(j, _, early=False):
        @pl.when(((y == 1) | (y == 2)) if early else (y >= 1))
        def _():
            down(total, j).wait_send()

        if not early:

            @pl.when((y == NY - 1) | (y == 0))
            def _():
                up(total, j).wait_send()

        return 0

    for j in range(EARLY):

        @pl.when(y >= 2)
        def _(j=j):
            raw_down(j).wait_send()

        @pl.when(y == NY - 1)
        def _(j=j):
            raw_up(j).wait_send()

    lax.fori_loop(0, EARLY, lambda j, _: sent(j, 0, True), 0)
    lax.fori_loop(EARLY, CHUNKS, sent, 0)
    pltpu.make_async_copy(got2, got2, red_send.at[1]).wait()
    lax.fori_loop(0, CHUNKS, finish_other, 0)


def per_device(krylov, adjoint, projected, stencil, column_weight, seam_turns):
    f32 = jnp.float32
    vm = pltpu.VMEM
    dma = pltpu.SemaphoreType.DMA
    part = vm((CHUNKS, PART, COLS), f32)
    raw = vm((EARLY, KRYLOV, PART, COLS), f32)
    sums = vm((KRYLOV, 2, HALF, COLS), f32)
    return pl.pallas_call(
        kernel,
        out_shape=jax.ShapeDtypeStruct(adjoint.shape, f32),
        in_specs=[pl.BlockSpec(memory_space=pltpu.HBM)] * 6,
        out_specs=pl.BlockSpec(memory_space=pltpu.VMEM),
        scratch_shapes=[
            vm(krylov.shape, krylov.dtype), vm(adjoint.shape, f32), vm(stencil.shape, stencil.dtype),
            vm(column_weight.shape, f32),
            pltpu.SMEM(projected.shape, f32), pltpu.SMEM(seam_turns.shape, jnp.int32),
            vm(stencil.shape, f32), vm((PAIRS, ROWS, COLS), f32),
            vm((PAIRS, COLS, COLS), jnp.bfloat16), vm((2 * LEVELS, COLS, COLS), jnp.bfloat16),
            sums, sums, sums, part, part, part, part, part, raw, raw, part, part,
            vm((1, COLS), f32), vm((1, COLS), f32),
            vm((len(FIRST), 1, COLS), f32), vm((len(SECOND), 1, COLS), f32),
            vm((2, STRIPS, COLS), f32), vm((2, STRIPS, COLS), f32), vm((2, 16, COLS), f32), vm((ROWS, COLS), f32),
            vm((COLS, COLS), f32), vm((2, STRIPS, ROWS), f32), vm((2, STRIPS, ROWS), f32), vm((2, 16, ROWS), f32),
            vm((2, COLS, COLS), f32), vm((ROWS, COLS), f32),
            dma((2 * FIELDS + 4,)), dma((2,)), dma((2,)), dma((2, KRYLOV)), dma((2, CHUNKS)), dma((CHUNKS,)),
            dma((CHUNKS,)), dma((2, EARLY)), dma((EARLY,)), dma((EARLY,)), dma((2, CHUNKS)), dma((8,)),
        ],
        name="step",
        compiler_params=pltpu.CompilerParams(
            collective_id=0, has_side_effects=True, vmem_limit_bytes=32 << 20
        ),
    )(
        *[
            pltpu.with_memory_space_constraint(a, pltpu.HBM)
            for a in (krylov, adjoint, stencil, column_weight, projected, seam_turns)
        ]
    )


def solution(mesh):
    placed = (
        P(None, "lev", None, "tile", None),
        P("lev", None, "tile", None),
        P(),
        P(None, "lev", "tile", None),
        P(None, "lev", "tile", None),
        P("tile", None),
    )
    return jax.shard_map(
        per_device,
        mesh=mesh,
        in_specs=placed,
        out_specs=P("lev", None, "tile", None),
        check_vma=False,
    )
```
